512 devices in a mesh: sx: 32 (over z_hi, x, y), sy: 16 (over z_lo, core).
Axes of the slice: x: 4, y: 4, z: 16 (z_hi: 2, z_lo: 8; z = z_hi * 8 + z_lo), core: 2. Of those that a mesh axis runs over, the one named last changes fastest.
Arguments:
- volume: bfloat16 [32, 512, 4096], P(None, 'sx', 'sy'), may hold values from -6 to 6
- w_first: bfloat16 [27, 32, 32], replicated, may hold values from -0.21875 to 0.21875
- down_weight: bfloat16 [2048, 128], replicated, may hold values from -0.125 to 0.125
- w_coarse: bfloat16 [4, 27, 128, 128], replicated, may hold values from -0.15625 to 0.15625
- w_up: bfloat16 [128, 2048], replicated, may hold values from -0.5 to 0.5
- closing_weight: bfloat16 [27, 32, 64], replicated, may hold values from -0.21875 to 0.21875
Outputs:
- result: bfloat16 [32, 512, 4096], P(None, 'sx', 'sy')
The draws below stay inside these ranges and needn't reach their ends.
All inputs are finite; a program needn't handle non-finite values.
Results may differ from the reference program's by a relative error of at most 0.0095.
Values may be sent and summed in bfloat16 or wider, within the bound.
No kernel may reach another device: no remote copies, remote signals or barrier semaphores. Data moves between devices by JAX's collectives and lax.ppermute only.
A program may use at most 64 MiB of HBM per device.

```python
import jax
import jax.numpy as jnp
from jax import lax

C = 32
CC = 128
LAYERS = 4
NZ = 16
NX = 512
NY = 256


def level_of(rng, dims, cuts, least, high):
    factor_of = 1.0
    for position, shards_of in cuts:
        heights = jax.random.uniform(jax.random.fold_in(jax.random.fold_in(rng, 6), position), (shards_of,), jnp.float32, least / len(cuts), high / len(cuts))
        factor_of = factor_of * jnp.repeat(jnp.exp(heights), dims[position] // shards_of).reshape((-1,) + (1,) * (len(dims) - 1 - position))
    return factor_of


def normal_values(key, extent, spread, limit, split=(), kind=jnp.bfloat16):
    values = spread * jax.random.normal(key, extent, jnp.float32)
    if split:
        values = values * level_of(key, extent, split, -0.22, 0.18)
    return jnp.clip(values, -limit, limit).astype(kind)


def setup_inputs(seed: int = 0) -> dict:
    keys = jax.random.split(jax.random.key(seed), 7)
    volume = normal_values(keys[0], (C, NX, NY * NZ), 1.0, 6.0, ((1, 32), (2, 16)))
    w_first = normal_values(keys[1], (27, C, C), (27 * C) ** -0.5, 0.21875)
    down_weight = normal_values(keys[2], (64 * C, CC), (64 * C) ** -0.5, 0.125)
    w_coarse = normal_values(keys[3], (LAYERS, 27, CC, CC), (27 * CC // 2) ** -0.5, 0.15625)
    w_up = normal_values(keys[4], (CC, 64 * C), CC ** -0.5, 0.5)
    closing_weight = normal_values(keys[5], (27, C, 2 * C), (27 * C) ** -0.5, 0.21875)
    return {"volume": volume, "w_first": w_first, "down_weight": down_weight, "w_coarse": w_coarse, "w_up": w_up, "closing_weight": closing_weight}


def conv_same(grid_field, weight):
    out_width = weight.shape[1]
    in_width = weight.shape[2]
    kernel = weight.astype(jnp.float32).reshape(3, 3, 3, out_width, in_width).transpose(3, 4, 0, 1, 2)
    summed = lax.conv_general_dilated(grid_field.astype(jnp.float32)[None], kernel, (1, 1, 1), ((1, 1), (1, 1), (1, 1)), dimension_numbers=("NCDHW", "OIDHW", "NCDHW"), precision=lax.Precision.HIGHEST)
    return summed[0]


def reference(volume, w_first, down_weight, w_coarse, w_up, closing_weight):
    grid_field = volume.reshape(C, NX, NY, NZ)
    skip_features = jax.nn.relu(conv_same(grid_field, w_first)).astype(jnp.bfloat16)
    blocks = skip_features.reshape(C, NX // 4, 4, NY // 4, 4, NZ // 4, 4).transpose(1, 3, 5, 0, 2, 4, 6).reshape(-1, C * 64)
    coarse_features = jnp.dot(blocks, down_weight, preferred_element_type=jnp.float32).astype(jnp.bfloat16)
    coarse_features = coarse_features.reshape(NX // 4, NY // 4, NZ // 4, CC).transpose(3, 0, 1, 2)
    for layer_index in range(LAYERS):
        coarse_features = jax.nn.relu(conv_same(coarse_features, w_coarse[layer_index])).astype(jnp.bfloat16)
    coarse_cells = coarse_features.transpose(1, 2, 3, 0).reshape(-1, CC)
    upsampled = jnp.dot(coarse_cells, w_up, preferred_element_type=jnp.float32).astype(jnp.bfloat16)
    upsampled = upsampled.reshape(NX // 4, NY // 4, NZ // 4, C, 4, 4, 4).transpose(3, 0, 4, 1, 5, 2, 6).reshape(C, NX, NY, NZ)
    joined = jnp.concatenate([skip_features, upsampled], axis=0)
    final = conv_same(joined, closing_weight).astype(jnp.bfloat16)
    return final.reshape(C, NX, NY * NZ)
```

```python
import jax
import jax.numpy as jnp
from jax import lax
from jax.experimental import pallas as pl
from jax.experimental.pallas import tpu as pltpu
from jax.sharding import PartitionSpec as P

NZ = 16
BF = jnp.bfloat16
F32 = jnp.float32
NT = (((1,), (1,)), ((), ()))
NN = (((1,), (0,)), ((), ()))
TN = (((0,), (0,)), ((), ()))


def iota(shape, dim):
    return lax.broadcasted_iota(jnp.int32, shape, dim)


def dot(a, b, dims):
    return lax.dot_general(a, b, dims, preferred_element_type=F32)


def z_shifts(value, rows):
    z = iota(value.shape, 0) & (NZ - 1)
    before = jnp.where(z == 0, 0.0, pltpu.roll(value, 1, 0))
    after = jnp.where(z == NZ - 1, 0.0, pltpu.roll(value, rows - 1, 0))
    return before, value, after


def regroup(rows, columns, row_dim, first):
    coarse = iota((rows, columns), row_dim)
    fine = iota((rows, columns), 1 - row_dim)
    offset = coarse >> 5
    y = 4 * (coarse & 7) + (offset >> 2)
    z = 4 * ((coarse >> 3) & 3) + (offset & 3)
    return jnp.where(fine == (y - first) * NZ + z, 1.0, 0.0).astype(BF)


def first_kernel(bounds, below, middle, above, w1, dwr, skip_ref, c0_ref, vz, grouped):
    for tile in range(7):
        lanes = slice(128 * tile, 128 * tile + 128)
        value = jnp.concatenate(
            [below[:, lanes].astype(F32), middle[:, lanes].astype(F32), above[:, lanes].astype(F32)], axis=0
        )
        for k, shifted in enumerate(z_shifts(value, 416)):
            vz[k, :, lanes] = shifted.astype(BF)
    to_groups = regroup(512, 384, 0, 0)
    y = (iota((384, 256), 0) >> 4) - 4
    lane = iota((384, 256), 1)
    y_inside = (y >= bounds[2]) & (y <= bounds[3])
    for g in range(3):
        summed = jnp.zeros((384, 256), F32)
        for oy in range(3):
            for oz in range(3):
                weight = jnp.concatenate([w1[0, 3 * oy + oz], w1[1, 3 * oy + oz]], axis=0)
                summed += dot(vz[oz, 16 * oy : 16 * oy + 384, 256 * g : 256 * g + 384], weight, NT)
        x = 8 * g - 4 + 4 * (lane >> 7) + (lane & 3)
        inside = y_inside & (x >= bounds[0]) & (x <= bounds[1])
        skip = jnp.where(inside, jnp.maximum(summed, 0.0), 0.0).astype(BF)
        skip_ref[:, 256 * g : 256 * g + 256] = skip
        grouped[:, 256 * g : 256 * g + 256] = dot(to_groups, skip, NN).astype(BF)
    coarse = jnp.zeros((192, 128), F32)
    for i in range(0, 16, 2):
        pieces = []
        for a in range(6):
            lanes = slice(128 * a, 128 * a + 128)
            pieces.append(
                jnp.concatenate([grouped[32 * i : 32 * i + 32, lanes], grouped[32 * i + 32 : 32 * i + 64, lanes]], axis=1)
            )
        coarse += dot(
            jnp.concatenate(pieces, axis=0), jnp.concatenate([dwr[i], dwr[i + 1]], axis=0), NN
        )
    for a in range(6):
        for z in range(4):
            c0_ref[a, :, 128 * z : 128 * z + 128] = coarse[32 * a + 8 * z : 32 * a + 8 * z + 8].astype(BF)


def closing_sum(values, weight, scratch, g):
    summed = jnp.zeros((256, 256), F32)
    for oy in range(3):
        for oz in range(3):
            summed += dot(
                weight[3 * oy + oz], scratch[oz, 16 * oy : 16 * oy + 256, 256 * g : 256 * g + 512], NT
            )
    return summed


def fill_shifts(value_of, scratch):
    for tile in range(6):
        lanes = slice(128 * tile, 128 * tile + 128)
        for k, shifted in enumerate(z_shifts(value_of(lanes), 288)):
            scratch[k, :, lanes] = shifted.astype(BF)


def skip_kernel(skip_ref, weight, out_ref, scratch):
    fill_shifts(lambda lanes: skip_ref[48:336, lanes].astype(F32), scratch)
    for g in range(2):
        out_ref[g] = closing_sum(None, weight, scratch, g)


def last_kernel(bounds, coarse_ref, w_coarse, wupr, weight, part_ref, out_ref, state, raw, up, scratch):
    value = coarse_ref[...].reshape(224, 512).astype(F32)
    for layer in range(4):
        rows_in = (14 - 2 * layer) * 16
        rows = rows_in - 32
        state[0, :rows_in] = value.astype(BF)
        state[1, :rows_in] = pltpu.roll(value, rows_in - 1, 0).astype(BF)
        state[2, :rows_in] = pltpu.roll(value, rows_in - 2, 0).astype(BF)
        low = jnp.zeros((rows, 256), F32)
        high = jnp.zeros((rows, 256), F32)
        zero = jnp.zeros((128, 128), BF)
        for oa in range(3):
            for ob in range(3):
                w = [w_coarse[layer, 9 * oa + 3 * ob + oz] for oz in range(3)]
                middle = jnp.concatenate(w, axis=1)
                w_low = jnp.concatenate([jnp.concatenate([w[1], w[2], zero], axis=1), middle], axis=0)
                w_high = jnp.concatenate([middle, jnp.concatenate([zero, w[0], w[1]], axis=1)], axis=0)
                low += dot(state[ob, 16 * oa : 16 * oa + rows, 0:384], w_low, NT)
                high += dot(state[ob, 16 * oa : 16 * oa + rows, 128:512], w_high, NT)
        index = iota((rows, 512), 0)
        a = (index >> 4) - 4 + layer
        b = index & 15
        kept = (a >= bounds[4]) & (a <= bounds[5]) & (b < 12 - 2 * layer)
        kept = kept & (b - 4 + layer >= bounds[6]) & (b - 4 + layer <= bounds[7])
        value = jnp.where(kept, jnp.maximum(jnp.concatenate([low, high], axis=1), 0.0), 0.0)
        value = value.astype(BF).astype(F32)
    cells = jnp.concatenate(
        [value[16 * a : 16 * a + 8, 128 * z : 128 * z + 128] for z in range(4) for a in range(6)], axis=0
    ).astype(BF)
    for i in range(0, 16, 2):
        pair = dot(cells, jnp.concatenate([wupr[i], wupr[i + 1]], axis=0), NT)
        for half in range(2):
            for z in range(4):
                for a in range(6):
                    raw[32 * (i + half) + 8 * z : 32 * (i + half) + 8 * z + 8, 128 * a : 128 * a + 128] = pair[
                        48 * z + 8 * a : 48 * z + 8 * a + 8, 128 * half : 128 * half + 128
                    ]
    from_groups = regroup(288, 512, 1, 3)
    for g in range(3):
        up[:, 256 * g : 256 * g + 256] = dot(from_groups, raw[:, 256 * g : 256 * g + 256].astype(BF), NN)
    fill_shifts(lambda lanes: up[:, lanes], scratch)
    for g in range(2):
        total = closing_sum(None, weight, scratch, g) + part_ref[g]
        out_ref[:, 8 * g : 8 * g + 8, :] = total.reshape(32, 8, 256).astype(BF)


VMEM = pl.BlockSpec(memory_space=pltpu.VMEM)
SMEM = pl.BlockSpec(memory_space=pltpu.SMEM)


def call(body, shapes, scratch, n_in, scalars, flops, limit):
    return pl.pallas_call(
        body,
        out_shape=[jax.ShapeDtypeStruct(s, t) for s, t in shapes],
        in_specs=([SMEM] if scalars else []) + [VMEM] * n_in,
        out_specs=[VMEM] * len(shapes),
        scratch_shapes=[pltpu.VMEM(s, t) for s, t in scratch],
        compiler_params=pltpu.CompilerParams(vmem_limit_bytes=limit << 20),
        cost_estimate=pl.CostEstimate(flops=flops, bytes_accessed=4 << 20, transcendentals=0),
        name=body.__name__,
    )


def ones_where(condition):
    return jnp.where(condition, 1.0, 0.0).astype(BF)


def place(rows, planes, shift):
    r, lane = iota((rows, 896), 0), iota((rows, 896), 1)
    return ones_where((lane & 31 == r // planes) & (lane >> 5 == r % planes + shift))


def taps(weight):
    out, width = weight.shape[1:]
    return weight.reshape(3, 9, out, width).transpose(1, 2, 0, 3).reshape(9, out, 3 * width)


def first_banded(weight):
    shape = (2, 4, 96, 384)
    xo = 4 * iota(shape, 0) + iota(shape, 1)
    d, k = iota(shape, 2), iota(shape, 3)
    select = ones_where((d & 31 == k & 31) & (k >> 5 == xo + (d >> 5)))
    banded = jnp.einsum("tod,axdk->atoxk", taps(weight), select, preferred_element_type=F32)
    return banded.astype(BF).reshape(2, 9, 128, 384)


def closing_banded(weight):
    shape = (8, 96, 512)
    xo, d, k = iota(shape, 0), iota(shape, 1), iota(shape, 2)
    select = ones_where((d & 31 == (k >> 2) & 31) & (4 * (k >> 7) + (k & 3) == xo + (d >> 5) + 3))
    banded = jnp.einsum("tod,xdk->toxk", taps(weight), select, preferred_element_type=F32)
    return banded.astype(BF).reshape(9, 256, 512)


def both_ways(array_up, array_down, axis):
    size = lax.axis_size(axis)
    up = [(i, i + 1) for i in range(size - 1)]
    down = [(j, i) for i, j in up]
    return lax.ppermute(array_up, axis, up), lax.ppermute(array_down, axis, down)


def local(volume, w_first, down_weight, w_coarse, w_up, closing_weight):
    ix, iy = lax.axis_index("sx"), lax.axis_index("sy")
    first_x, last_x = ix == 0, ix == lax.axis_size("sx") - 1
    first_y, last_y = iy == 0, iy == lax.axis_size("sy") - 1
    bounds = jnp.stack(
        [
            jnp.where(first_x, 0, -99),
            jnp.where(last_x, 15, 99),
            jnp.where(first_y, 0, -99),
            jnp.where(last_y, 15, 99),
            jnp.where(first_x, 0, -99),
            jnp.where(last_x, 3, 99),
            jnp.where(first_y, 0, -99),
            jnp.where(last_y, 3, 99),
        ]
    ).astype(jnp.int32)
    left, right = both_ways(volume[:, 8:16], volume[:, 0:8], "sx")
    rows = dot(volume.reshape(512, 256), place(512, 16, 5), TN)
    rows = rows + dot(left.reshape(256, 256), place(256, 8, -3), TN)
    rows = (rows + dot(right.reshape(256, 256), place(256, 8, 21), TN)).astype(BF)
    below, above = both_ways(rows[176:256], rows[0:80], "sy")
    skip, coarse = call(
        first_kernel,
        [((384, 768), BF), ((6, 8, 512), BF)],
        [((3, 416, 896), BF), ((512, 768), BF)],
        5,
        True,
        2 << 30,
        24,
    )(
        bounds,
        below,
        rows,
        above,
        first_banded(w_first),
        down_weight.reshape(128, 16, 128).transpose(1, 0, 2),
    )
    (part,) = call(skip_kernel, [((2, 256, 256), F32)], [((3, 288, 768), BF)], 2, False, 2 << 30, 16)(
        skip, closing_banded(closing_weight[:, :, :32])
    )
    before, after = both_ways(coarse[:, 0:4], coarse[:, 2:6], "sy")
    coarse = jnp.concatenate([before, coarse[:, 0:6], after, jnp.zeros((6, 2, 512), BF)], axis=1)
    before, after = both_ways(coarse[0:4], coarse[2:6], "sx")
    coarse = jnp.concatenate([before, coarse, after], axis=0)
    w_up_rows = lax.optimization_barrier(w_up.T).reshape(128, 16, 128).transpose(1, 0, 2)
    (result,) = call(
        last_kernel,
        [((32, 16, 256), BF)],
        [((3, 224, 512), BF), ((512, 768), F32), ((288, 768), F32), ((3, 288, 768), BF)],
        5,
        True,
        3 << 30,
        32,
    )(bounds, coarse, w_coarse, w_up_rows, closing_banded(closing_weight[:, :, 32:]), part)
    return result


def solution(mesh):
    return jax.shard_map(
        local,
        mesh=mesh,
        in_specs=(P(None, "sx", "sy"), P(), P(), P(), P(), P()),
        out_specs=P(None, "sx", "sy"),
        check_vma=False,
    )
```

```python
import jax
import jax.numpy as jnp
from jax import lax
from jax.experimental import pallas as pl
from jax.experimental.pallas import tpu as pltpu
from jax.sharding import PartitionSpec as P

NZ = 16
BF = jnp.bfloat16
F32 = jnp.float32
NT = (((1,), (1,)), ((), ()))
NN = (((1,), (0,)), ((), ()))
TN = (((0,), (0,)), ((), ()))


def iota(shape, dim):
    return lax.broadcasted_iota(jnp.int32, shape, dim)


def dot(a, b, dims):
    return lax.dot_general(a, b, dims, preferred_element_type=F32)


def z_shifts(value, rows):
    z = iota(value.shape, 0) & (NZ - 1)
    before = jnp.where(z == 0, 0.0, pltpu.roll(value, 1, 0))
    after = jnp.where(z == NZ - 1, 0.0, pltpu.roll(value, rows - 1, 0))
    return before, value, after


def regroup(rows, columns, row_dim, first):
    coarse = iota((rows, columns), row_dim)
    fine = iota((rows, columns), 1 - row_dim)
    offset = coarse >> 5
    y = 4 * (coarse & 7) + (offset >> 2)
    z = 4 * ((coarse >> 3) & 3) + (offset & 3)
    return jnp.where(fine == (y - first) * NZ + z, 1.0, 0.0).astype(BF)


def first_kernel(bounds, below, middle, above, w1, dwr, skip_ref, c0_ref, vz, grouped):
    for tile in range(7):
        lanes = slice(128 * tile, 128 * tile + 128)
        value = jnp.concatenate(
            [below[:, lanes].astype(F32), middle[:, lanes].astype(F32), above[:, lanes].astype(F32)], axis=0
        )
        for k, shifted in enumerate(z_shifts(value, 416)):
            vz[k, :, lanes] = shifted.astype(BF)
    to_groups = regroup(512, 384, 0, 0)
    y = (iota((384, 256), 0) >> 4) - 4
    lane = iota((384, 256), 1)
    y_inside = (y >= bounds[2]) & (y <= bounds[3])
    for g in range(3):
        summed = jnp.zeros((384, 256), F32)
        for oy in range(3):
            for oz in range(3):
                weight = jnp.concatenate([w1[0, 3 * oy + oz], w1[1, 3 * oy + oz]], axis=0)
                summed += dot(vz[oz, 16 * oy : 16 * oy + 384, 256 * g : 256 * g + 384], weight, NT)
        x = 8 * g - 4 + 4 * (lane >> 7) + (lane & 3)
        inside = y_inside & (x >= bounds[0]) & (x <= bounds[1])
        skip = jnp.where(inside, jnp.maximum(summed, 0.0), 0.0).astype(BF)
        skip_ref[:, 256 * g : 256 * g + 256] = skip
        grouped[:, 256 * g : 256 * g + 256] = dot(to_groups, skip, NN).astype(BF)
    coarse = jnp.zeros((192, 128), F32)
    for i in range(0, 16, 2):
        pieces = []
        for a in range(6):
            lanes = slice(128 * a, 128 * a + 128)
            pieces.append(
                jnp.concatenate([grouped[32 * i : 32 * i + 32, lanes], grouped[32 * i + 32 : 32 * i + 64, lanes]], axis=1)
            )
        coarse += dot(
            jnp.concatenate(pieces, axis=0), jnp.concatenate([dwr[i], dwr[i + 1]], axis=0), NN
        )
    for a in range(6):
        for z in range(4):
            c0_ref[a, :, 128 * z : 128 * z + 128] = coarse[32 * a + 8 * z : 32 * a + 8 * z + 8].astype(BF)


def closing_sum(weight, scratch, g):
    summed = jnp.zeros((256, 256), F32)
    for oy in range(3):
        for oz in range(3):
            summed += dot(
                weight[3 * oy + oz], scratch[oz, 16 * oy : 16 * oy + 256, 256 * g : 256 * g + 512], NT
            )
    return summed


def fill_shifts(value_of, scratch):
    for tile in range(6):
        lanes = slice(128 * tile, 128 * tile + 128)
        for k, shifted in enumerate(z_shifts(value_of(lanes), 288)):
            scratch[k, :, lanes] = shifted.astype(BF)


def skip_kernel(skip_ref, weight, out_ref, scratch):
    fill_shifts(lambda lanes: skip_ref[48:336, lanes].astype(F32), scratch)
    for g in range(2):
        out_ref[g] = closing_sum(weight, scratch, g)


def last_kernel(bounds, coarse_ref, w_hbm, wupr, weight, part_ref, out_ref, state, raw, up, scratch, w_coarse, arrived):
    copies = [pltpu.make_async_copy(w_hbm.at[k], w_coarse.at[k], arrived.at[k]) for k in range(4)]
    for copy in copies:
        copy.start()
    value = coarse_ref[...].reshape(224, 512).astype(F32)
    for layer in range(4):
        rows_in = (14 - 2 * layer) * 16
        rows = rows_in - 32
        state[0, :rows_in] = value.astype(BF)
        state[1, :rows_in] = pltpu.roll(value, rows_in - 1, 0).astype(BF)
        state[2, :rows_in] = pltpu.roll(value, rows_in - 2, 0).astype(BF)
        low = jnp.zeros((rows, 256), F32)
        high = jnp.zeros((rows, 256), F32)
        zero = jnp.zeros((128, 128), BF)
        copies[layer].wait()
        for oa in range(3):
            for ob in range(3):
                w = [w_coarse[layer, 9 * oa + 3 * ob + oz] for oz in range(3)]
                middle = jnp.concatenate(w, axis=1)
                w_low = jnp.concatenate([jnp.concatenate([w[1], w[2], zero], axis=1), middle], axis=0)
                w_high = jnp.concatenate([middle, jnp.concatenate([zero, w[0], w[1]], axis=1)], axis=0)
                low += dot(state[ob, 16 * oa : 16 * oa + rows, 0:384], w_low, NT)
                high += dot(state[ob, 16 * oa : 16 * oa + rows, 128:512], w_high, NT)
        index = iota((rows, 512), 0)
        a = (index >> 4) - 4 + layer
        b = index & 15
        kept = (a >= bounds[4]) & (a <= bounds[5]) & (b < 12 - 2 * layer)
        kept = kept & (b - 4 + layer >= bounds[6]) & (b - 4 + layer <= bounds[7])
        value = jnp.where(kept, jnp.maximum(jnp.concatenate([low, high], axis=1), 0.0), 0.0)
        value = value.astype(BF).astype(F32)
    cells = jnp.concatenate(
        [value[16 * a : 16 * a + 8, 128 * z : 128 * z + 128] for z in range(4) for a in range(6)], axis=0
    ).astype(BF)
    for i in range(0, 16, 2):
        pair = dot(cells, jnp.concatenate([wupr[i], wupr[i + 1]], axis=0), NT)
        for half in range(2):
            for z in range(4):
                for a in range(6):
                    raw[32 * (i + half) + 8 * z : 32 * (i + half) + 8 * z + 8, 128 * a : 128 * a + 128] = pair[
                        48 * z + 8 * a : 48 * z + 8 * a + 8, 128 * half : 128 * half + 128
                    ]
    from_groups = regroup(288, 512, 1, 3)
    for g in range(3):
        up[:, 256 * g : 256 * g + 256] = dot(from_groups, raw[:, 256 * g : 256 * g + 256].astype(BF), NN)
    fill_shifts(lambda lanes: up[:, lanes], scratch)
    row, column = iota((256, 256), 0), iota((256, 256), 1)
    to_channels = jnp.where(column == ((row & 7) << 5) + (row >> 3), 1.0, 0.0).astype(BF)
    for g in range(2):
        total = (closing_sum(weight, scratch, g) + part_ref[g]).astype(BF)
        out_ref[:, 8 * g : 8 * g + 8, :] = dot(to_channels, total, NN).reshape(32, 8, 256).astype(BF)


VMEM = pl.BlockSpec(memory_space=pltpu.VMEM)
SMEM = pl.BlockSpec(memory_space=pltpu.SMEM)


def call(body, shapes, scratch, n_in, scalars, flops, limit, in_hbm=(), semaphores=()):
    return pl.pallas_call(
        body,
        out_shape=[jax.ShapeDtypeStruct(s, t) for s, t in shapes],
        in_specs=([SMEM] if scalars else []) + [pl.BlockSpec(memory_space=pl.ANY) if k in in_hbm else VMEM for k in range(n_in)],
        out_specs=[VMEM] * len(shapes),
        scratch_shapes=[pltpu.VMEM(s, t) for s, t in scratch] + list(semaphores),
        compiler_params=pltpu.CompilerParams(vmem_limit_bytes=limit << 20),
        cost_estimate=pl.CostEstimate(flops=flops, bytes_accessed=4 << 20, transcendentals=0),
    )


def ones_where(condition):
    return jnp.where(condition, 1.0, 0.0).astype(BF)


def chosen_planes(odd):
    row, column = iota((320, 512), 0), iota((320, 512), 1)
    second = row >= 160
    inner = jnp.where(second, row - 160, row)
    plane = (inner >> 5) + jnp.where(second != odd, 11, 0)
    return ones_where((column >> 4 == inner & 31) & (column & 15 == plane))


def place_own():
    r, lane = iota((512, 896), 0), iota((512, 896), 1)
    return ones_where((lane & 31 == r >> 4) & (lane >> 5 == (r & 15) + 5))


def place_halo(at_right):
    r, lane = iota((160, 896), 0), iota((160, 896), 1)
    return ones_where(lane == r + jnp.where(at_right, 672, 0))


def taps(weight):
    out, width = weight.shape[1:]
    return weight.reshape(3, 9, out, width).transpose(1, 2, 0, 3).reshape(9, out, 3 * width)


def first_banded(weight):
    shape = (2, 4, 96, 384)
    xo = 4 * iota(shape, 0) + iota(shape, 1)
    d, k = iota(shape, 2), iota(shape, 3)
    select = ones_where((d & 31 == k & 31) & (k >> 5 == xo + (d >> 5)))
    banded = jnp.einsum("tod,axdk->atoxk", taps(weight), select, preferred_element_type=F32)
    return banded.astype(BF).reshape(2, 9, 128, 384)


def closing_banded(weight):
    shape = (8, 96, 512)
    xo, d, k = iota(shape, 0), iota(shape, 1), iota(shape, 2)
    select = ones_where((d & 31 == (k >> 2) & 31) & (4 * (k >> 7) + (k & 3) == xo + (d >> 5) + 3))
    banded = jnp.einsum("tod,xdk->txok", taps(weight), select, preferred_element_type=F32)
    return banded.astype(BF).reshape(9, 256, 512)


def both_ways(array_up, array_down, axis):
    size = lax.axis_size(axis)
    up = [(i, i + 1) for i in range(size - 1)]
    down = [(j, i) for i, j in up]
    return lax.ppermute(array_up, axis, up), lax.ppermute(array_down, axis, down)


def swaps(first, second, axis):
    size = lax.axis_size(axis)
    received = []
    for array, start in ((first, 1), (second, 0)):
        pairs = [(i, i + 1) for i in range(start, size - 1, 2)]
        received.append(lax.ppermute(array, axis, pairs + [(j, i) for i, j in pairs]))
    return received


def local(volume, w_first, down_weight, w_coarse, w_up, closing_weight):
    ix, iy = lax.axis_index("sx"), lax.axis_index("sy")
    first_x, last_x = ix == 0, ix == lax.axis_size("sx") - 1
    first_y, last_y = iy == 0, iy == lax.axis_size("sy") - 1
    bounds = jnp.stack(
        [
            jnp.where(first_x, 0, -99),
            jnp.where(last_x, 15, 99),
            jnp.where(first_y, 0, -99),
            jnp.where(last_y, 15, 99),
            jnp.where(first_x, 0, -99),
            jnp.where(last_x, 3, 99),
            jnp.where(first_y, 0, -99),
            jnp.where(last_y, 3, 99),
        ]
    ).astype(jnp.int32)
    odd = (ix & 1) == 1
    flat = volume.reshape(512, 256)
    payload = dot(chosen_planes(odd), flat, NN).astype(BF)
    far, near = swaps(payload[:160], payload[160:], "sx")
    rows = dot(flat, place_own(), TN) + dot(near, place_halo(~odd), TN)
    prepared = (
        rows,
        place_halo(odd),
        first_banded(w_first),
        down_weight.reshape(128, 16, 128).transpose(1, 0, 2),
        closing_banded(closing_weight[:, :, :32]),
        closing_banded(closing_weight[:, :, 32:]),
        lax.optimization_barrier(w_up.T).reshape(128, 16, 128).transpose(1, 0, 2),
    )
    far, prepared = lax.optimization_barrier((far, prepared))
    rows, far_place, w1, dwr, skip_weight, up_weight, wupr = prepared
    rows = (rows + dot(far, far_place, TN)).astype(BF)
    below, above = both_ways(rows[176:256], rows[0:80], "sy")
    skip, coarse = call(
        first_kernel,
        [((384, 768), BF), ((6, 8, 512), BF)],
        [((3, 416, 896), BF), ((512, 768), BF)],
        5,
        True,
        2 << 30,
        24,
    )(bounds, below, rows, above, w1, dwr)
    lower, upper = coarse[0:4], coarse[2:6]
    far, near = swaps(jnp.where(odd, lower, upper), jnp.where(odd, upper, lower), "sx")
    (part,) = call(skip_kernel, [((2, 256, 256), F32)], [((3, 288, 768), BF)], 2, False, 2 << 30, 16)(skip, skip_weight)
    coarse = jnp.concatenate([jnp.where(odd, near, far), coarse, jnp.where(odd, far, near)], axis=0)
    before, after = both_ways(coarse[:, 0:4], coarse[:, 2:6], "sy")
    coarse = jnp.concatenate([before, coarse[:, 0:6], after, jnp.zeros((14, 2, 512), BF)], axis=1)
    (result,) = call(
        last_kernel,
        [((32, 16, 256), BF)],
        [
            ((3, 224, 512), BF),
            ((512, 768), F32),
            ((288, 768), F32),
            ((3, 288, 768), BF),
            ((4, 27, 128, 128), BF),
        ],
        5,
        True,
        3 << 30,
        32,
        in_hbm=(1,),
        semaphores=(pltpu.SemaphoreType.DMA((4,)),),
    )(bounds, coarse, w_coarse, wupr, up_weight, part)
    return result


def solution(mesh):
    return jax.shard_map(
        local,
        mesh=mesh,
        in_specs=(P(None, "sx", "sy"), P(), P(), P(), P(), P()),
        out_specs=P(None, "sx", "sy"),
        check_vma=False,
    )
```

```python
import jax
import jax.numpy as jnp
from jax import lax
from jax.experimental import pallas as pl
from jax.experimental.pallas import tpu as pltpu
from jax.sharding import PartitionSpec as P

NZ = 16
BF = jnp.bfloat16
F32 = jnp.float32
NT = (((1,), (1,)), ((), ()))
NN = (((1,), (0,)), ((), ()))
TN = (((0,), (0,)), ((), ()))


def iota(shape, dim):
    return lax.broadcasted_iota(jnp.int32, shape, dim)


def dot(a, b, dims):
    return lax.dot_general(a, b, dims, preferred_element_type=F32)


def z_shifts(value, rows):
    z = iota(value.shape, 0) & (NZ - 1)
    before = jnp.where(z == 0, 0.0, pltpu.roll(value, 1, 0))
    after = jnp.where(z == NZ - 1, 0.0, pltpu.roll(value, rows - 1, 0))
    return before, value, after


def regroup(rows, columns, row_dim, first):
    coarse = iota((rows, columns), row_dim)
    fine = iota((rows, columns), 1 - row_dim)
    offset = coarse >> 5
    y = 4 * (coarse & 7) + (offset >> 2)
    z = 4 * ((coarse >> 3) & 3) + (offset & 3)
    return jnp.where(fine == (y - first) * NZ + z, 1.0, 0.0).astype(BF)


def first_kernel(bounds, below, middle, above, w1, dwr, skip_ref, c0_ref, vz, grouped):
    for tile in range(7):
        lanes = slice(128 * tile, 128 * tile + 128)
        value = jnp.concatenate(
            [below[:, lanes].astype(F32), middle[:, lanes].astype(F32), above[:, lanes].astype(F32)], axis=0
        )
        for k, shifted in enumerate(z_shifts(value, 416)):
            vz[k, :, lanes] = shifted.astype(BF)
    to_groups = regroup(512, 384, 0, 0)
    y = (iota((384, 256), 0) >> 4) - 4
    lane = iota((384, 256), 1)
    y_inside = (y >= bounds[2]) & (y <= bounds[3])
    for g in range(3):
        summed = jnp.zeros((384, 256), F32)
        for oy in range(3):
            for oz in range(3):
                summed += dot(
                    vz[oz, 16 * oy : 16 * oy + 384, 256 * g : 256 * g + 384], w1[3 * oy + oz], NT
                )
        x = 8 * g - 4 + (lane >> 5)
        inside = y_inside & (x >= bounds[0]) & (x <= bounds[1])
        skip = jnp.where(inside, jnp.maximum(summed, 0.0), 0.0).astype(BF)
        skip_ref[:, 256 * g : 256 * g + 256] = skip
        grouped[:, 256 * g : 256 * g + 256] = dot(to_groups, skip, NN).astype(BF)
    coarse = jnp.zeros((192, 128), F32)
    for i in range(0, 16, 2):
        pieces = []
        for a in range(6):
            lanes = slice(128 * a, 128 * a + 128)
            pieces.append(
                jnp.concatenate([grouped[32 * i : 32 * i + 32, lanes], grouped[32 * i + 32 : 32 * i + 64, lanes]], axis=1)
            )
        coarse += dot(
            jnp.concatenate(pieces, axis=0), jnp.concatenate([dwr[i], dwr[i + 1]], axis=0), NN
        )
    for a in range(6):
        for z in range(4):
            c0_ref[a, :, 128 * z : 128 * z + 128] = coarse[32 * a + 8 * z : 32 * a + 8 * z + 8].astype(BF)


def closing_sum(weight, scratch, g):
    summed = jnp.zeros((256, 256), F32)
    for oy in range(3):
        for oz in range(3):
            summed += dot(
                weight[3 * oy + oz], scratch[oz, 16 * oy : 16 * oy + 256, 256 * g : 256 * g + 512], NT
            )
    return summed


def fill_shifts(value_of, scratch):
    for tile in range(6):
        lanes = slice(128 * tile, 128 * tile + 128)
        for k, shifted in enumerate(z_shifts(value_of(lanes), 288)):
            scratch[k, :, lanes] = shifted.astype(BF)


def skip_kernel(skip_ref, weight, out_ref, scratch):
    fill_shifts(lambda lanes: skip_ref[48:336, lanes].astype(F32), scratch)
    for g in range(2):
        out_ref[g] = closing_sum(weight, scratch, g)


def last_kernel(bounds, coarse_ref, w_coarse, wupr, weight, part_ref, out_ref, state, raw, up, scratch):
    value = coarse_ref[...].reshape(224, 512).astype(F32)
    for layer in range(4):
        rows_in = (14 - 2 * layer) * 16
        rows = rows_in - 32
        state[0, :rows_in] = value.astype(BF)
        state[1, :rows_in] = pltpu.roll(value, rows_in - 1, 0).astype(BF)
        state[2, :rows_in] = pltpu.roll(value, rows_in - 2, 0).astype(BF)
        low = jnp.zeros((rows, 256), F32)
        high = jnp.zeros((rows, 256), F32)
        zero = jnp.zeros((128, 128), BF)
        for oa in range(3):
            for ob in range(3):
                w = [w_coarse[layer, 9 * oa + 3 * ob + oz] for oz in range(3)]
                middle = jnp.concatenate(w, axis=1)
                w_low = jnp.concatenate([jnp.concatenate([w[1], w[2], zero], axis=1), middle], axis=0)
                w_high = jnp.concatenate([middle, jnp.concatenate([zero, w[0], w[1]], axis=1)], axis=0)
                low += dot(state[ob, 16 * oa : 16 * oa + rows, 0:384], w_low, NT)
                high += dot(state[ob, 16 * oa : 16 * oa + rows, 128:512], w_high, NT)
        index = iota((rows, 512), 0)
        a = (index >> 4) - 4 + layer
        b = index & 15
        kept = (a >= bounds[4]) & (a <= bounds[5]) & (b < 12 - 2 * layer)
        kept = kept & (b - 4 + layer >= bounds[6]) & (b - 4 + layer <= bounds[7])
        value = jnp.where(kept, jnp.maximum(jnp.concatenate([low, high], axis=1), 0.0), 0.0)
        value = value.astype(BF).astype(F32)
    cells = jnp.concatenate(
        [value[16 * a : 16 * a + 8, 128 * z : 128 * z + 128] for z in range(4) for a in range(6)], axis=0
    ).astype(BF)
    for i in range(0, 16, 2):
        pair = dot(cells, jnp.concatenate([wupr[i], wupr[i + 1]], axis=0), NT)
        for half in range(2):
            for z in range(4):
                for a in range(6):
                    raw[32 * (i + half) + 8 * z : 32 * (i + half) + 8 * z + 8, 128 * a : 128 * a + 128] = pair[
                        48 * z + 8 * a : 48 * z + 8 * a + 8, 128 * half : 128 * half + 128
                    ]
    from_groups = regroup(288, 512, 1, 3)
    for g in range(3):
        up[:, 256 * g : 256 * g + 256] = dot(from_groups, raw[:, 256 * g : 256 * g + 256].astype(BF), NN)
    fill_shifts(lambda lanes: up[:, lanes], scratch)
    row, column = iota((256, 256), 0), iota((256, 256), 1)
    to_channels = jnp.where(column == ((row & 7) << 5) + (row >> 3), 1.0, 0.0).astype(BF)
    for g in range(2):
        total = (closing_sum(weight, scratch, g) + part_ref[g]).astype(BF)
        out_ref[:, 8 * g : 8 * g + 8, :] = dot(to_channels, total, NN).reshape(32, 8, 256).astype(BF)


def prepare_kernel(first, closing, down, up, w1, skip_weight, up_weight, dwr, wupr, tall):
    for source, target, width, shift, channels in (
        (first, w1, 384, 0, 0),
        (closing, skip_weight, 512, 3, 0),
        (closing, up_weight, 512, 3, 32),
    ):
        inputs = source.shape[2]
        repeat = iota((inputs, width), 0) - channels == iota((inputs, width), 1) & 31
        repeat = jnp.where(repeat, 1.0, 0.0).astype(BF)
        plane = (iota((32, width), 1) >> 5) - shift
        for t in range(9):
            tiled = dot(jnp.concatenate([source[t], source[t + 9], source[t + 18]], axis=0), repeat, NN)
            for x in range(8):
                banded = jnp.where(plane == x + 2, tiled[64:], 0.0)
                banded = jnp.where(plane == x + 1, tiled[32:64], banded)
                banded = jnp.where(plane == x, tiled[:32], banded)
                target[t, 32 * x : 32 * x + 32] = banded.astype(BF)
    for source, target in ((down, dwr), (up, wupr)):
        if source is down:
            tall[...] = down[...].astype(F32)
        else:
            for k in range(16):
                tall[128 * k : 128 * k + 128] = up[:, 128 * k : 128 * k + 128].astype(F32).T
        for i in range(16):
            for x in range(4):
                target[i, 32 * x : 32 * x + 32] = tall[pl.ds(16 * x + i, 32, stride=64), :].astype(BF)


VMEM = pl.BlockSpec(memory_space=pltpu.VMEM)
SMEM = pl.BlockSpec(memory_space=pltpu.SMEM)


def call(body, shapes, scratch, n_in, scalars, flops, limit):
    return pl.pallas_call(
        body,
        out_shape=[jax.ShapeDtypeStruct(s, t) for s, t in shapes],
        in_specs=([SMEM] if scalars else []) + [VMEM] * n_in,
        out_specs=[VMEM] * len(shapes),
        scratch_shapes=[pltpu.VMEM(s, t) for s, t in scratch],
        compiler_params=pltpu.CompilerParams(vmem_limit_bytes=limit << 20),
        cost_estimate=pl.CostEstimate(flops=flops, bytes_accessed=4 << 20, transcendentals=0),
    )


def ones_where(condition):
    return jnp.where(condition, 1.0, 0.0).astype(BF)


def chosen_planes(upper):
    row, column = iota((160, 512), 0), iota((160, 512), 1)
    plane = (row >> 5) + jnp.where(upper, 11, 0)
    return ones_where((column >> 4 == row & 31) & (column & 15 == plane))


def place_own():
    r, lane = iota((512, 896), 0), iota((512, 896), 1)
    return ones_where((lane & 31 == r >> 4) & (lane >> 5 == (r & 15) + 5))


def place_halo(at_right):
    r, lane = iota((160, 896), 0), iota((160, 896), 1)
    return ones_where(lane == r + jnp.where(at_right, 672, 0))


def both_ways(array_up, array_down, axis):
    size = lax.axis_size(axis)
    up = [(i, i + 1) for i in range(size - 1)]
    down = [(j, i) for i, j in up]
    return lax.ppermute(array_up, axis, up), lax.ppermute(array_down, axis, down)


def swaps(first, second, axis):
    size = lax.axis_size(axis)
    received = []
    for array, start in ((first, 1), (second, 0)):
        pairs = [(i, i + 1) for i in range(start, size - 1, 2)]
        received.append(lax.ppermute(array, axis, pairs + [(j, i) for i, j in pairs]))
    return received


def local(volume, w_first, down_weight, w_coarse, w_up, closing_weight):
    ix, iy = lax.axis_index("sx"), lax.axis_index("sy")
    first_x, last_x = ix == 0, ix == lax.axis_size("sx") - 1
    first_y, last_y = iy == 0, iy == lax.axis_size("sy") - 1
    bounds = jnp.stack(
        [
            jnp.where(first_x, 0, -99),
            jnp.where(last_x, 15, 99),
            jnp.where(first_y, 0, -99),
            jnp.where(last_y, 15, 99),
            jnp.where(first_x, 0, -99),
            jnp.where(last_x, 3, 99),
            jnp.where(first_y, 0, -99),
            jnp.where(last_y, 3, 99),
        ]
    ).astype(jnp.int32)
    odd = (ix & 1) == 1
    flat = volume.reshape(512, 256)
    payload = [dot(chosen_planes(side), flat, NN).astype(BF) for side in (odd, ~odd)]
    far, near = swaps(*payload, "sx")
    rows = dot(flat, place_own(), TN) + dot(near, place_halo(~odd), TN)
    weights = call(
        prepare_kernel,
        [((9, 256, 384), BF), ((9, 256, 512), BF), ((9, 256, 512), BF), ((16, 128, 128), BF), ((16, 128, 128), BF)],
        [((2048, 128), F32)],
        4,
        False,
        1 << 28,
        24,
    )(w_first, closing_weight, down_weight, w_up)
    far, rows, far_place, weights = lax.optimization_barrier((far, rows, place_halo(odd), weights))
    w1, skip_weight, up_weight, dwr, wupr = weights
    rows = (rows + dot(far, far_place, TN)).astype(BF)
    below, above = both_ways(rows[176:256], rows[0:80], "sy")
    skip, coarse = call(
        first_kernel,
        [((384, 768), BF), ((6, 8, 512), BF)],
        [((3, 416, 896), BF), ((512, 768), BF)],
        5,
        True,
        2 << 30,
        24,
    )(bounds, below, rows, above, w1, dwr)
    lower, upper = coarse[0:4], coarse[2:6]
    far, near = swaps(jnp.where(odd, lower, upper), jnp.where(odd, upper, lower), "sx")
    (part,) = call(skip_kernel, [((2, 256, 256), F32)], [((3, 288, 768), BF)], 2, False, 2 << 30, 16)(skip, skip_weight)
    coarse = jnp.concatenate([jnp.where(odd, near, far), coarse, jnp.where(odd, far, near)], axis=0)
    before, after = both_ways(coarse[:, 0:4], coarse[:, 2:6], "sy")
    coarse = jnp.concatenate([before, coarse[:, 0:6], after, jnp.zeros((14, 2, 512), BF)], axis=1)
    (result,) = call(
        last_kernel,
        [((32, 16, 256), BF)],
        [
            ((3, 224, 512), BF),
            ((512, 768), F32),
            ((288, 768), F32),
            ((3, 288, 768), BF),
        ],
        5,
        True,
        3 << 30,
        32,
    )(bounds, coarse, w_coarse, wupr, up_weight, part)
    return result


def solution(mesh):
    return jax.shard_map(
        local,
        mesh=mesh,
        in_specs=(P(None, "sx", "sy"), P(), P(), P(), P(), P()),
        out_specs=P(None, "sx", "sy"),
        check_vma=False,
    )
```

```python
import jax
import jax.numpy as jnp
from jax import lax
from jax.experimental import pallas as pl
from jax.experimental.pallas import tpu as pltpu
from jax.sharding import PartitionSpec as P

NZ = 16
BF = jnp.bfloat16
F32 = jnp.float32
NT = (((1,), (1,)), ((), ()))
NN = (((1,), (0,)), ((), ()))
TN = (((0,), (0,)), ((), ()))


def iota(shape, dim):
    return lax.broadcasted_iota(jnp.int32, shape, dim)


def dot(a, b, dims):
    return lax.dot_general(a, b, dims, preferred_element_type=F32)


def z_shifts(value, rows):
    z = iota(value.shape, 0) & (NZ - 1)
    before = jnp.where(z == 0, 0.0, pltpu.roll(value, 1, 0))
    after = jnp.where(z == NZ - 1, 0.0, pltpu.roll(value, rows - 1, 0))
    return before, value, after


def regroup(rows, columns, row_dim, first):
    coarse = iota((rows, columns), row_dim)
    fine = iota((rows, columns), 1 - row_dim)
    offset = coarse >> 5
    y = 4 * (coarse & 7) + (offset >> 2)
    z = 4 * ((coarse >> 3) & 3) + (offset & 3)
    return jnp.where(fine == (y - first) * NZ + z, 1.0, 0.0).astype(BF)


def side_window(own, halo, halo_at_left, lanes):
    tile = lanes.start // 128
    other = slice(128 * (tile ^ 2), 128 * (tile ^ 2) + 128)
    here = slice(128 * (tile & 1), 128 * (tile & 1) + 128)
    outer, inner = halo[:, here].astype(F32), own[:, other].astype(F32)
    return jnp.where(halo_at_left, outer, inner) if tile < 2 else jnp.where(halo_at_left, inner, outer)


def fine_groups(windows, bounds, w1, dwr, skip_refs, coarse_refs, vz, grouped):
    to_groups = regroup(512, 384, 0, 0)
    y = (iota((384, 256), 0) >> 4) - 4
    plane = iota((384, 256), 1) >> 5
    y_inside = (y >= bounds[2]) & (y <= bounds[3])
    for k, (window, first_x) in enumerate(windows):
        for tile in range(4):
            lanes = slice(128 * tile, 128 * tile + 128)
            for oz, shifted in enumerate(z_shifts(window(lanes), 416)):
                vz[oz, :, lanes] = shifted.astype(BF)
        summed = jnp.zeros((384, 256), F32)
        for oy in range(3):
            for oz in range(3):
                summed += dot(vz[oz, 16 * oy : 16 * oy + 384], w1[3 * oy + oz], NT)
        x = plane + first_x
        inside = y_inside & (x >= bounds[0]) & (x <= bounds[1])
        skip = jnp.where(inside, jnp.maximum(summed, 0.0), 0.0).astype(BF)
        skip_refs[k][...] = skip
        grouped[:, 256 * k : 256 * k + 256] = dot(to_groups, skip, NN).astype(BF)
    count = 2 * len(windows)
    coarse = jnp.zeros((32 * count, 128), F32)
    for i in range(0, 16, 2):
        pieces = []
        for a in range(count):
            lanes = slice(128 * a, 128 * a + 128)
            pieces.append(
                jnp.concatenate([grouped[32 * i : 32 * i + 32, lanes], grouped[32 * i + 32 : 32 * i + 64, lanes]], axis=1)
            )
        coarse += dot(
            jnp.concatenate(pieces, axis=0), jnp.concatenate([dwr[i], dwr[i + 1]], axis=0), NN
        )
    for a in range(count):
        for target, first_a in coarse_refs[a // 2]:
            for z in range(4):
                cell = coarse[32 * a + 8 * z : 32 * a + 8 * z + 8].astype(BF)
                target[first_a + a % 2, :, 128 * z : 128 * z + 128] = cell


def near_kernel(bounds, own, near, w1, dwr, skip_near, skip_own, to_far, coarse_own, vz, grouped):
    odd = bounds[8] == 1
    first_near, first_own = 2 - 2 * bounds[8], 2 * bounds[8]
    windows = (
        (lambda lanes: side_window(own, near, odd, lanes), jnp.where(odd, -4, 12)),
        (lambda lanes: own[:, lanes].astype(F32), 4),
    )
    coarse = ([(to_far, first_near)], [(to_far, first_own), (coarse_own, 0)])
    fine_groups(windows, bounds, w1, dwr, (skip_near, skip_own), coarse, vz, grouped)


def far_kernel(bounds, own, far, w1, dwr, coarse_own, skip_far, to_near, vz, grouped):
    to_near[pl.ds(2 - 2 * bounds[8], 2)] = coarse_own[...]
    even = bounds[8] == 0
    windows = ((lambda lanes: side_window(own, far, even, lanes), jnp.where(even, -4, 12)),)
    fine_groups(windows, bounds, w1, dwr, (skip_far,), ([(to_near, 2 * bounds[8])],), vz, grouped)


def closing_sum(weight, scratch, g):
    summed = jnp.zeros((256, 256), F32)
    for oy in range(3):
        for oz in range(3):
            summed += dot(
                weight[3 * oy + oz], scratch[oz, 16 * oy : 16 * oy + 256, 256 * g : 256 * g + 512], NT
            )
    return summed


def fill_shifts(value_of, scratch):
    for tile in range(6):
        lanes = slice(128 * tile, 128 * tile + 128)
        for k, shifted in enumerate(z_shifts(value_of(lanes), 288)):
            scratch[k, :, lanes] = shifted.astype(BF)


def skip_kernel(bounds, near, own, far, weight, out_ref, scratch):
    odd = bounds[8] == 1

    def value_of(lanes):
        group, half = divmod(lanes.start // 128, 2)
        here = slice(128 * half, 128 * half + 128)
        if group == 1:
            return own[48:336, here].astype(F32)
        first, second = near[48:336, here].astype(F32), far[48:336, here].astype(F32)
        return jnp.where(odd, first, second) if group == 0 else jnp.where(odd, second, first)

    fill_shifts(value_of, scratch)
    for g in range(2):
        out_ref[g] = closing_sum(weight, scratch, g)


def last_kernel(bounds, coarse_ref, w_coarse, wupr, weight, part_ref, out_ref, state, raw, up, scratch):
    value = coarse_ref[...].reshape(224, 512).astype(F32)
    for layer in range(4):
        rows_in = (14 - 2 * layer) * 16
        rows = rows_in - 32
        state[0, :rows_in] = value.astype(BF)
        state[1, :rows_in] = pltpu.roll(value, rows_in - 1, 0).astype(BF)
        state[2, :rows_in] = pltpu.roll(value, rows_in - 2, 0).astype(BF)
        low = jnp.zeros((rows, 256), F32)
        high = jnp.zeros((rows, 256), F32)
        zero = jnp.zeros((128, 128), BF)
        for oa in range(3):
            for ob in range(3):
                w = [w_coarse[layer, 9 * oa + 3 * ob + oz] for oz in range(3)]
                middle = jnp.concatenate(w, axis=1)
                w_low = jnp.concatenate([jnp.concatenate([w[1], w[2], zero], axis=1), middle], axis=0)
                w_high = jnp.concatenate([middle, jnp.concatenate([zero, w[0], w[1]], axis=1)], axis=0)
                low += dot(state[ob, 16 * oa : 16 * oa + rows, 0:384], w_low, NT)
                high += dot(state[ob, 16 * oa : 16 * oa + rows, 128:512], w_high, NT)
        index = iota((rows, 512), 0)
        a = (index >> 4) - 4 + layer
        b = index & 15
        kept = (a >= bounds[4]) & (a <= bounds[5]) & (b < 12 - 2 * layer)
        kept = kept & (b - 4 + layer >= bounds[6]) & (b - 4 + layer <= bounds[7])
        value = jnp.where(kept, jnp.maximum(jnp.concatenate([low, high], axis=1), 0.0), 0.0)
        value = value.astype(BF).astype(F32)
    cells = jnp.concatenate(
        [value[16 * a : 16 * a + 8, 128 * z : 128 * z + 128] for z in range(4) for a in range(6)], axis=0
    ).astype(BF)
    for i in range(0, 16, 2):
        pair = dot(cells, jnp.concatenate([wupr[i], wupr[i + 1]], axis=0), NT)
        for half in range(2):
            for z in range(4):
                for a in range(6):
                    raw[32 * (i + half) + 8 * z : 32 * (i + half) + 8 * z + 8, 128 * a : 128 * a + 128] = pair[
                        48 * z + 8 * a : 48 * z + 8 * a + 8, 128 * half : 128 * half + 128
                    ]
    from_groups = regroup(288, 512, 1, 3)
    for g in range(3):
        up[:, 256 * g : 256 * g + 256] = dot(from_groups, raw[:, 256 * g : 256 * g + 256].astype(BF), NN)
    fill_shifts(lambda lanes: up[:, lanes], scratch)
    row, column = iota((256, 256), 0), iota((256, 256), 1)
    to_channels = jnp.where(column == ((row & 7) << 5) + (row >> 3), 1.0, 0.0).astype(BF)
    for g in range(2):
        total = (closing_sum(weight, scratch, g) + part_ref[g]).astype(BF)
        out_ref[:, 8 * g : 8 * g + 8, :] = dot(to_channels, total, NN).reshape(32, 8, 256).astype(BF)


def banded(source, target, channels):
    inputs = source.shape[2]
    repeat = iota((inputs, 512), 0) - channels == iota((inputs, 512), 1) & 31
    repeat = jnp.where(repeat, 1.0, 0.0).astype(BF)
    plane = (iota((32, 512), 1) >> 5) - 3
    for t in range(9):
        tiled = dot(jnp.concatenate([source[t], source[t + 9], source[t + 18]], axis=0), repeat, NN)
        for x in range(8):
            rows = jnp.where(plane == x + 2, tiled[64:], 0.0)
            rows = jnp.where(plane == x + 1, tiled[32:64], rows)
            rows = jnp.where(plane == x, tiled[:32], rows)
            target[t, 32 * x : 32 * x + 32] = rows.astype(BF)


def by_offset(tall, target):
    for i in range(16):
        for x in range(4):
            target[i, 32 * x : 32 * x + 32] = tall[pl.ds(16 * x + i, 32, stride=64), :].astype(BF)


def prepare_first_kernel(first, down, w1, dwr, tall):
    banded(first, w1, 0)
    tall[...] = down[...].astype(F32)
    by_offset(tall, dwr)


def prepare_last_kernel(closing, up, skip_weight, up_weight, wupr, tall):
    banded(closing, skip_weight, 0)
    banded(closing, up_weight, 32)
    for k in range(16):
        tall[128 * k : 128 * k + 128] = up[:, 128 * k : 128 * k + 128].astype(F32).T
    by_offset(tall, wupr)


VMEM = pl.BlockSpec(memory_space=pltpu.VMEM)
SMEM = pl.BlockSpec(memory_space=pltpu.SMEM)


def call(body, shapes, scratch, n_in, scalars, flops, limit):
    return pl.pallas_call(
        body,
        out_shape=[jax.ShapeDtypeStruct(s, t) for s, t in shapes],
        in_specs=([SMEM] if scalars else []) + [VMEM] * n_in,
        out_specs=[VMEM] * len(shapes),
        scratch_shapes=[pltpu.VMEM(s, t) for s, t in scratch],
        compiler_params=pltpu.CompilerParams(vmem_limit_bytes=limit << 20),
        cost_estimate=pl.CostEstimate(flops=flops, bytes_accessed=4 << 20, transcendentals=0),
    )


def ones_where(condition):
    return jnp.where(condition, 1.0, 0.0).astype(BF)


def place_own():
    r, lane = iota((512, 512), 0), iota((512, 512), 1)
    return ones_where((lane & 31 == r >> 4) & (lane >> 5 == r & 15))


def both_ways(array_up, array_down, axis):
    size = lax.axis_size(axis)
    up = [(i, i + 1) for i in range(size - 1)]
    down = [(j, i) for i, j in up]
    return lax.ppermute(array_up, axis, up), lax.ppermute(array_down, axis, down)


def swap(array, axis, start):
    pairs = [(i, i + 1) for i in range(start, lax.axis_size(axis) - 1, 2)]
    return lax.ppermute(array, axis, pairs + [(j, i) for i, j in pairs])


def swaps(first, second, axis):
    return swap(first, axis, 1), swap(second, axis, 0)


def local(volume, w_first, down_weight, w_coarse, w_up, closing_weight):
    ix, iy = lax.axis_index("sx"), lax.axis_index("sy")
    first_x, last_x = ix == 0, ix == lax.axis_size("sx") - 1
    first_y, last_y = iy == 0, iy == lax.axis_size("sy") - 1
    bounds = jnp.stack(
        [
            jnp.where(first_x, 0, -99),
            jnp.where(last_x, 15, 99),
            jnp.where(first_y, 0, -99),
            jnp.where(last_y, 15, 99),
            jnp.where(first_x, 0, -99),
            jnp.where(last_x, 3, 99),
            jnp.where(first_y, 0, -99),
            jnp.where(last_y, 3, 99),
            ix & 1,
        ]
    ).astype(jnp.int32)
    odd = (ix & 1) == 1
    own = dot(volume.reshape(512, 256), place_own(), TN).astype(BF)
    below, above = both_ways(own[176:256], own[0:80], "sy")
    own = jnp.concatenate([below, own, above], axis=0)
    left, right = own[:, :256], own[:, 256:]
    far, near = swaps(jnp.where(odd, right, left), jnp.where(odd, left, right), "sx")
    w1, dwr = call(
        prepare_first_kernel, [((9, 256, 512), BF), ((16, 128, 128), BF)], [((2048, 128), F32)], 2, False, 1 << 27, 12
    )(w_first, down_weight)
    skip, cells = ((384, 256), BF), ((4, 8, 512), BF)
    skip_near, skip_own, to_far, coarse_own = call(
        near_kernel,
        [skip, skip, cells, ((2, 8, 512), BF)],
        [((3, 416, 512), BF), ((512, 512), BF)],
        4,
        True,
        2 << 30,
        24,
    )(bounds, own, near, w1, dwr)
    far_cells = swap(to_far, "sx", 1)
    skip_far, to_near = call(
        far_kernel, [skip, cells], [((3, 416, 512), BF), ((512, 256), BF)], 5, True, 1 << 30, 24
    )(bounds, own, far, w1, dwr, coarse_own)
    near_cells = swap(to_near, "sx", 0)
    skip_weight, up_weight, wupr = call(
        prepare_last_kernel,
        [((9, 256, 512), BF), ((9, 256, 512), BF), ((16, 128, 128), BF)],
        [((2048, 128), F32)],
        2,
        False,
        1 << 28,
        16,
    )(closing_weight, w_up)
    (part,) = call(skip_kernel, [((2, 256, 256), F32)], [((3, 288, 768), BF)], 4, True, 2 << 30, 16)(
        bounds, skip_near, skip_own, skip_far, skip_weight
    )
    odd_order = jnp.concatenate([near_cells, to_far[:2], to_near, far_cells], axis=0)
    even_order = jnp.concatenate([far_cells, to_near, to_far[2:], near_cells], axis=0)
    coarse = jnp.where(odd, odd_order, even_order)
    before, after = both_ways(coarse[:, 0:4], coarse[:, 2:6], "sy")
    coarse = jnp.concatenate([before, coarse[:, 0:6], after, jnp.zeros((14, 2, 512), BF)], axis=1)
    (result,) = call(
        last_kernel,
        [((32, 16, 256), BF)],
        [
            ((3, 224, 512), BF),
            ((512, 768), F32),
            ((288, 768), F32),
            ((3, 288, 768), BF),
        ],
        5,
        True,
        3 << 30,
        32,
    )(bounds, coarse, w_coarse, wupr, up_weight, part)
    return result


def solution(mesh):
    return jax.shard_map(
        local,
        mesh=mesh,
        in_specs=(P(None, "sx", "sy"), P(), P(), P(), P(), P()),
        out_specs=P(None, "sx", "sy"),
        check_vma=False,
    )
```

```python
import jax
import jax.numpy as jnp
from jax import lax
from jax.experimental import pallas as pl
from jax.experimental.pallas import tpu as pltpu
from jax.sharding import PartitionSpec as P

NZ = 16
BF = jnp.bfloat16
F32 = jnp.float32
NT = (((1,), (1,)), ((), ()))
NN = (((1,), (0,)), ((), ()))
TN = (((0,), (0,)), ((), ()))


def iota(shape, dim):
    return lax.broadcasted_iota(jnp.int32, shape, dim)


def dot(a, b, dims):
    return lax.dot_general(a, b, dims, preferred_element_type=F32)


def z_shifts(value, rows):
    z = iota(value.shape, 0) & (NZ - 1)
    before = jnp.where(z == 0, 0.0, pltpu.roll(value, 1, 0))
    after = jnp.where(z == NZ - 1, 0.0, pltpu.roll(value, rows - 1, 0))
    return before, value, after


def regroup(rows, columns, row_dim, first):
    coarse = iota((rows, columns), row_dim)
    fine = iota((rows, columns), 1 - row_dim)
    offset = coarse >> 5
    y = 4 * (coarse & 7) + (offset >> 2)
    z = 4 * ((coarse >> 3) & 3) + (offset & 3)
    return jnp.where(fine == (y - first) * NZ + z, 1.0, 0.0).astype(BF)


def side_window(own, halo, halo_at_left, lanes):
    tile = lanes.start // 128
    other = slice(128 * (tile ^ 2), 128 * (tile ^ 2) + 128)
    here = slice(128 * (tile & 1), 128 * (tile & 1) + 128)
    outer, inner = halo[:, here].astype(F32), own[:, other].astype(F32)
    return jnp.where(halo_at_left, outer, inner) if tile < 2 else jnp.where(halo_at_left, inner, outer)


def fine_groups(windows, bounds, w1, dwr, skip_refs, coarse_refs, vz, grouped):
    to_groups = regroup(512, 384, 0, 0)
    y = (iota((384, 256), 0) >> 4) - 4
    plane = iota((384, 256), 1) >> 5
    y_inside = (y >= bounds[2]) & (y <= bounds[3])
    for k, (window, first_x) in enumerate(windows):
        for tile in range(4):
            lanes = slice(128 * tile, 128 * tile + 128)
            for oz, shifted in enumerate(z_shifts(window(lanes), 416)):
                vz[oz, :, lanes] = shifted.astype(BF)
        summed = jnp.zeros((384, 256), F32)
        for oy in range(3):
            for oz in range(3):
                summed += dot(vz[oz, 16 * oy : 16 * oy + 384], w1[3 * oy + oz], NT)
        x = plane + first_x
        inside = y_inside & (x >= bounds[0]) & (x <= bounds[1])
        skip = jnp.where(inside, jnp.maximum(summed, 0.0), 0.0).astype(BF)
        skip_refs[k][...] = skip
        grouped[:, 256 * k : 256 * k + 256] = dot(to_groups, skip, NN).astype(BF)
    count = 2 * len(windows)
    coarse = jnp.zeros((32 * count, 128), F32)
    for i in range(0, 16, 2):
        pieces = []
        for a in range(count):
            lanes = slice(128 * a, 128 * a + 128)
            pieces.append(
                jnp.concatenate([grouped[32 * i : 32 * i + 32, lanes], grouped[32 * i + 32 : 32 * i + 64, lanes]], axis=1)
            )
        coarse += dot(
            jnp.concatenate(pieces, axis=0), jnp.concatenate([dwr[i], dwr[i + 1]], axis=0), NN
        )
    for a in range(count):
        for target, first_a in coarse_refs[a // 2]:
            for z in range(4):
                cell = coarse[32 * a + 8 * z : 32 * a + 8 * z + 8].astype(BF)
                target[first_a + a % 2, :, 128 * z : 128 * z + 128] = cell


def near_kernel(bounds, own, near, w1, dwr, skip_near, skip_own, to_far, coarse_own, vz, grouped):
    odd = bounds[8] == 1
    first_near, first_own = 2 - 2 * bounds[8], 2 * bounds[8]
    windows = (
        (lambda lanes: side_window(own, near, odd, lanes), jnp.where(odd, -4, 12)),
        (lambda lanes: own[:, lanes].astype(F32), 4),
    )
    coarse = ([(to_far, first_near)], [(to_far, first_own), (coarse_own, 0)])
    fine_groups(windows, bounds, w1, dwr, (skip_near, skip_own), coarse, vz, grouped)


def far_kernel(bounds, own, far, w1, dwr, coarse_own, skip_far, to_near, vz, grouped):
    to_near[pl.ds(2 - 2 * bounds[8], 2)] = coarse_own[...]
    even = bounds[8] == 0
    windows = ((lambda lanes: side_window(own, far, even, lanes), jnp.where(even, -4, 12)),)
    fine_groups(windows, bounds, w1, dwr, (skip_far,), ([(to_near, 2 * bounds[8])],), vz, grouped)


def closing_sum(weight, scratch, g):
    summed = jnp.zeros((256, 256), F32)
    for oy in range(3):
        for oz in range(3):
            summed += dot(
                weight[3 * oy + oz], scratch[oz, 16 * oy : 16 * oy + 256, 256 * g : 256 * g + 512], NT
            )
    return summed


def fill_shifts(value_of, scratch):
    for tile in range(6):
        lanes = slice(128 * tile, 128 * tile + 128)
        for k, shifted in enumerate(z_shifts(value_of(lanes), 288)):
            scratch[k, :, lanes] = shifted.astype(BF)


def skip_kernel(bounds, near, own, far, weight, out_ref, scratch):
    odd = bounds[8] == 1

    def value_of(lanes):
        group, half = divmod(lanes.start // 128, 2)
        here = slice(128 * half, 128 * half + 128)
        if group == 1:
            return own[48:336, here].astype(F32)
        first, second = near[48:336, here].astype(F32), far[48:336, here].astype(F32)
        return jnp.where(odd, first, second) if group == 0 else jnp.where(odd, second, first)

    fill_shifts(value_of, scratch)
    for g in range(2):
        out_ref[g] = closing_sum(weight, scratch, g)


def last_kernel(bounds, coarse_ref, w_coarse, wupr, weight, part_ref, out_ref, state, raw, up, scratch):
    value = coarse_ref[...].reshape(224, 512).astype(F32)
    for layer in range(4):
        rows_in = (14 - 2 * layer) * 16
        rows = rows_in - 32
        state[0, :rows_in] = value.astype(BF)
        state[1, :rows_in] = pltpu.roll(value, rows_in - 1, 0).astype(BF)
        state[2, :rows_in] = pltpu.roll(value, rows_in - 2, 0).astype(BF)
        low = jnp.zeros((rows, 256), F32)
        high = jnp.zeros((rows, 256), F32)
        zero = jnp.zeros((128, 128), BF)
        for oa in range(3):
            for ob in range(3):
                w = [w_coarse[layer, 9 * oa + 3 * ob + oz] for oz in range(3)]
                middle = jnp.concatenate(w, axis=1)
                w_low = jnp.concatenate([jnp.concatenate([w[1], w[2], zero], axis=1), middle], axis=0)
                w_high = jnp.concatenate([middle, jnp.concatenate([zero, w[0], w[1]], axis=1)], axis=0)
                low += dot(state[ob, 16 * oa : 16 * oa + rows, 0:384], w_low, NT)
                high += dot(state[ob, 16 * oa : 16 * oa + rows, 128:512], w_high, NT)
        index = iota((rows, 512), 0)
        a = (index >> 4) - 4 + layer
        b = index & 15
        kept = (a >= bounds[4]) & (a <= bounds[5]) & (b < 12 - 2 * layer)
        kept = kept & (b - 4 + layer >= bounds[6]) & (b - 4 + layer <= bounds[7])
        value = jnp.where(kept, jnp.maximum(jnp.concatenate([low, high], axis=1), 0.0), 0.0)
        value = value.astype(BF).astype(F32)
    cells = jnp.concatenate(
        [value[16 * a : 16 * a + 8, 128 * z : 128 * z + 128] for z in range(4) for a in range(6)], axis=0
    ).astype(BF)
    for i in range(0, 16, 2):
        pair = dot(cells, jnp.concatenate([wupr[i], wupr[i + 1]], axis=0), NT)
        for half in range(2):
            for z in range(4):
                for a in range(6):
                    raw[32 * (i + half) + 8 * z : 32 * (i + half) + 8 * z + 8, 128 * a : 128 * a + 128] = pair[
                        48 * z + 8 * a : 48 * z + 8 * a + 8, 128 * half : 128 * half + 128
                    ]
    from_groups = regroup(288, 512, 1, 3)
    for g in range(3):
        up[:, 256 * g : 256 * g + 256] = dot(from_groups, raw[:, 256 * g : 256 * g + 256].astype(BF), NN)
    fill_shifts(lambda lanes: up[:, lanes], scratch)
    row, column = iota((256, 256), 0), iota((256, 256), 1)
    to_channels = jnp.where(column == ((row & 7) << 5) + (row >> 3), 1.0, 0.0).astype(BF)
    for g in range(2):
        total = (closing_sum(weight, scratch, g) + part_ref[g]).astype(BF)
        out_ref[:, 8 * g : 8 * g + 8, :] = dot(to_channels, total, NN).reshape(32, 8, 256).astype(BF)


def banded(source, target, channels):
    inputs = source.shape[2]
    repeat = iota((inputs, 512), 0) - channels == iota((inputs, 512), 1) & 31
    repeat = jnp.where(repeat, 1.0, 0.0).astype(BF)
    plane = (iota((32, 512), 1) >> 5) - 3
    for t in range(9):
        tiled = dot(jnp.concatenate([source[t], source[t + 9], source[t + 18]], axis=0), repeat, NN)
        for x in range(8):
            rows = jnp.where(plane == x + 2, tiled[64:], 0.0)
            rows = jnp.where(plane == x + 1, tiled[32:64], rows)
            rows = jnp.where(plane == x, tiled[:32], rows)
            target[t, 32 * x : 32 * x + 32] = rows.astype(BF)


def by_offset(tall, target):
    for i in range(16):
        for x in range(4):
            target[i, 32 * x : 32 * x + 32] = tall[pl.ds(16 * x + i, 32, stride=64), :].astype(BF)


def prepare_first_kernel(first, down, w1, dwr, tall):
    banded(first, w1, 0)
    tall[...] = down[...].astype(F32)
    by_offset(tall, dwr)


def prepare_last_kernel(closing, up, skip_weight, up_weight, wupr, tall):
    banded(closing, skip_weight, 0)
    banded(closing, up_weight, 32)
    for k in range(16):
        tall[128 * k : 128 * k + 128] = up[:, 128 * k : 128 * k + 128].astype(F32).T
    by_offset(tall, wupr)


VMEM = pl.BlockSpec(memory_space=pltpu.VMEM)
SMEM = pl.BlockSpec(memory_space=pltpu.SMEM)


def call(body, shapes, scratch, n_in, scalars, flops, limit):
    return pl.pallas_call(
        body,
        out_shape=[jax.ShapeDtypeStruct(s, t) for s, t in shapes],
        in_specs=([SMEM] if scalars else []) + [VMEM] * n_in,
        out_specs=[VMEM] * len(shapes),
        scratch_shapes=[pltpu.VMEM(s, t) for s, t in scratch],
        compiler_params=pltpu.CompilerParams(vmem_limit_bytes=limit << 20),
        cost_estimate=pl.CostEstimate(flops=flops, bytes_accessed=4 << 20, transcendentals=0),
    )


def ones_where(condition):
    return jnp.where(condition, 1.0, 0.0).astype(BF)


def place_own():
    r, lane = iota((512, 512), 0), iota((512, 512), 1)
    return ones_where((lane & 31 == r >> 4) & (lane >> 5 == r & 15))


def swap(array, axis, start):
    pairs = [(i, i + 1) for i in range(start, lax.axis_size(axis) - 1, 2)]
    return lax.ppermute(array, axis, pairs + [(j, i) for i, j in pairs])


def y_neighbours(bottom, top, odd_y):
    chips = swap(jnp.where(odd_y, top, bottom), "sy", 1)
    cores = swap(jnp.where(odd_y, bottom, top), "sy", 0)
    return jnp.where(odd_y, cores, chips), jnp.where(odd_y, chips, cores)


def local(volume, w_first, down_weight, w_coarse, w_up, closing_weight):
    ix, iy = lax.axis_index("sx"), lax.axis_index("sy")
    first_x, last_x = ix == 0, ix == lax.axis_size("sx") - 1
    first_y, last_y = iy == 0, iy == lax.axis_size("sy") - 1
    bounds = jnp.stack(
        [
            jnp.where(first_x, 0, -99),
            jnp.where(last_x, 15, 99),
            jnp.where(first_y, 0, -99),
            jnp.where(last_y, 15, 99),
            jnp.where(first_x, 0, -99),
            jnp.where(last_x, 3, 99),
            jnp.where(first_y, 0, -99),
            jnp.where(last_y, 3, 99),
            ix & 1,
        ]
    ).astype(jnp.int32)
    odd = (ix & 1) == 1
    own = dot(volume.reshape(512, 256), place_own(), TN).astype(BF)
    odd_y = (iy & 1) == 1
    below, above = y_neighbours(own[0:80], own[176:256], odd_y)
    own = jnp.concatenate([below, own, above], axis=0)
    left, right = own[:, :256], own[:, 256:]
    near = swap(jnp.where(odd, left, right), "sx", 0)
    far = swap(jnp.where(odd, right, left), "sx", 1)
    w1, dwr = call(
        prepare_first_kernel, [((9, 256, 512), BF), ((16, 128, 128), BF)], [((2048, 128), F32)], 2, False, 1 << 27, 12
    )(w_first, down_weight)
    skip, cells = ((384, 256), BF), ((4, 8, 512), BF)
    skip_near, skip_own, to_far, coarse_own = call(
        near_kernel,
        [skip, skip, cells, ((2, 8, 512), BF)],
        [((3, 416, 512), BF), ((512, 512), BF)],
        4,
        True,
        2 << 30,
        24,
    )(bounds, own, near, w1, dwr)
    far_cells = swap(to_far, "sx", 1)
    skip_far, to_near = call(
        far_kernel, [skip, cells], [((3, 416, 512), BF), ((512, 256), BF)], 5, True, 1 << 30, 24
    )(bounds, own, far, w1, dwr, coarse_own)
    near_cells = swap(to_near, "sx", 0)
    skip_weight, up_weight, wupr = call(
        prepare_last_kernel,
        [((9, 256, 512), BF), ((9, 256, 512), BF), ((16, 128, 128), BF)],
        [((2048, 128), F32)],
        2,
        False,
        1 << 28,
        16,
    )(closing_weight, w_up)
    (part,) = call(skip_kernel, [((2, 256, 256), F32)], [((3, 288, 768), BF)], 4, True, 2 << 30, 16)(
        bounds, skip_near, skip_own, skip_far, skip_weight
    )
    odd_order = jnp.concatenate([near_cells, to_far[:2], to_near, far_cells], axis=0)
    even_order = jnp.concatenate([far_cells, to_near, to_far[2:], near_cells], axis=0)
    coarse = jnp.where(odd, odd_order, even_order)
    before, after = y_neighbours(coarse[:, 2:6], coarse[:, 0:4], odd_y)
    coarse = jnp.concatenate([before, coarse[:, 0:6], after, jnp.zeros((14, 2, 512), BF)], axis=1)
    (result,) = call(
        last_kernel,
        [((32, 16, 256), BF)],
        [
            ((3, 224, 512), BF),
            ((512, 768), F32),
            ((288, 768), F32),
            ((3, 288, 768), BF),
        ],
        5,
        True,
        3 << 30,
        32,
    )(bounds, coarse, w_coarse, wupr, up_weight, part)
    return result


def solution(mesh):
    return jax.shard_map(
        local,
        mesh=mesh,
        in_specs=(P(None, "sx", "sy"), P(), P(), P(), P(), P()),
        out_specs=P(None, "sx", "sy"),
        check_vma=False,
    )
```

```python
import jax
import jax.numpy as jnp
from jax import lax
from jax.experimental import pallas as pl
from jax.experimental.pallas import tpu as pltpu
from jax.sharding import PartitionSpec as P

NZ = 16
BF = jnp.bfloat16
F32 = jnp.float32
NT = (((1,), (1,)), ((), ()))
NN = (((1,), (0,)), ((), ()))
TN = (((0,), (0,)), ((), ()))


def iota(shape, dim):
    return lax.broadcasted_iota(jnp.int32, shape, dim)


def dot(a, b, dims):
    return lax.dot_general(a, b, dims, preferred_element_type=F32)


def z_shifts(value, rows):
    z = iota(value.shape, 0) & (NZ - 1)
    before = jnp.where(z == 0, 0.0, pltpu.roll(value, 1, 0))
    after = jnp.where(z == NZ - 1, 0.0, pltpu.roll(value, rows - 1, 0))
    return before, value, after


def regroup(rows, columns, row_dim, first):
    coarse = iota((rows, columns), row_dim)
    fine = iota((rows, columns), 1 - row_dim)
    offset = coarse >> 5
    y = 4 * (coarse & 7) + (offset >> 2)
    z = 4 * ((coarse >> 3) & 3) + (offset & 3)
    return jnp.where(fine == (y - first) * NZ + z, 1.0, 0.0).astype(BF)


def moved(value, start, target):
    lane = iota(value.shape, 1)
    return jnp.where(lane >> 5 == target // 32, pltpu.roll(value, (target - start) % 128, 1), 0.0)


def packed(joined, tile, fifth_tile, start):
    fifth = joined[:, 128 * fifth_tile : 128 * fifth_tile + 128]
    blocks = [moved(fifth[104 * k : 104 * k + 104], start, 32 * k) for k in range(4)]
    return jnp.concatenate(
        [joined[:, 128 * tile : 128 * tile + 128], (blocks[0] + blocks[1]) + (blocks[2] + blocks[3])], axis=0
    )


def pack_kernel(bounds, own, chips, cores, joined_ref, to_near, to_far):
    odd, odd_y = bounds[8] == 1, bounds[9] == 1
    chip, core = chips[...].astype(F32), cores[...].astype(F32)
    joined = jnp.concatenate(
        [jnp.where(odd_y, core, chip), own[...].astype(F32), jnp.where(odd_y, chip, core)], axis=0
    )
    joined_ref[...] = joined.astype(BF)
    left, right = packed(joined, 0, 1, 0), packed(joined, 3, 2, 96)
    to_far[...] = jnp.where(odd, right, left).astype(BF)
    to_near[...] = jnp.where(odd, left, right).astype(BF)


def side_window(own, halo, halo_at_left, lanes):
    tile = lanes.start // 128
    other = slice(128 * (tile ^ 2), 128 * (tile ^ 2) + 128)
    inner = own[:, other].astype(F32)
    if tile in (1, 2):
        outer = halo[0:416].astype(F32)
    else:
        fifth = halo[416:520].astype(F32)
        outer = jnp.concatenate([moved(fifth, 32 * k, 96 if tile == 0 else 0) for k in range(4)], axis=0)
    return jnp.where(halo_at_left, outer, inner) if tile < 2 else jnp.where(halo_at_left, inner, outer)


def fine_groups(windows, bounds, w1, dwr, skip_refs, coarse_refs, vz, grouped):
    to_groups = regroup(512, 384, 0, 0)
    y = (iota((384, 256), 0) >> 4) - 4
    plane = iota((384, 256), 1) >> 5
    y_inside = (y >= bounds[2]) & (y <= bounds[3])
    for k, (window, first_x) in enumerate(windows):
        for tile in range(4):
            lanes = slice(128 * tile, 128 * tile + 128)
            for oz, shifted in enumerate(z_shifts(window(lanes), 416)):
                vz[oz, :, lanes] = shifted.astype(BF)
        summed = jnp.zeros((384, 256), F32)
        for oy in range(3):
            for oz in range(3):
                summed += dot(vz[oz, 16 * oy : 16 * oy + 384], w1[3 * oy + oz], NT)
        x = plane + first_x
        inside = y_inside & (x >= bounds[0]) & (x <= bounds[1])
        skip = jnp.where(inside, jnp.maximum(summed, 0.0), 0.0).astype(BF)
        skip_refs[k][...] = skip
        grouped[:, 256 * k : 256 * k + 256] = dot(to_groups, skip, NN).astype(BF)
    count = 2 * len(windows)
    coarse = jnp.zeros((32 * count, 128), F32)
    for i in range(0, 16, 2):
        pieces = []
        for a in range(count):
            lanes = slice(128 * a, 128 * a + 128)
            pieces.append(
                jnp.concatenate([grouped[32 * i : 32 * i + 32, lanes], grouped[32 * i + 32 : 32 * i + 64, lanes]], axis=1)
            )
        coarse += dot(
            jnp.concatenate(pieces, axis=0), jnp.concatenate([dwr[i], dwr[i + 1]], axis=0), NN
        )
    for a in range(count):
        for target, first_a in coarse_refs[a // 2]:
            for z in range(4):
                cell = coarse[32 * a + 8 * z : 32 * a + 8 * z + 8].astype(BF)
                target[first_a + a % 2, :, 128 * z : 128 * z + 128] = cell


def near_kernel(bounds, own, near, w1, dwr, skip_near, skip_own, to_far, coarse_own, vz, grouped):
    odd = bounds[8] == 1
    first_near, first_own = 2 - 2 * bounds[8], 2 * bounds[8]
    windows = (
        (lambda lanes: side_window(own, near, odd, lanes), jnp.where(odd, -4, 12)),
        (lambda lanes: own[:, lanes].astype(F32), 4),
    )
    coarse = ([(to_far, first_near)], [(to_far, first_own), (coarse_own, 0)])
    fine_groups(windows, bounds, w1, dwr, (skip_near, skip_own), coarse, vz, grouped)


def far_kernel(bounds, own, far, w1, dwr, coarse_own, skip_far, to_near, vz, grouped):
    to_near[pl.ds(2 - 2 * bounds[8], 2)] = coarse_own[...]
    even = bounds[8] == 0
    windows = ((lambda lanes: side_window(own, far, even, lanes), jnp.where(even, -4, 12)),)
    fine_groups(windows, bounds, w1, dwr, (skip_far,), ([(to_near, 2 * bounds[8])],), vz, grouped)


def closing_sum(weight, scratch, g):
    summed = jnp.zeros((256, 256), F32)
    for oy in range(3):
        for oz in range(3):
            summed += dot(
                weight[3 * oy + oz], scratch[oz, 16 * oy : 16 * oy + 256, 256 * g : 256 * g + 512], NT
            )
    return summed


def fill_shifts(value_of, scratch):
    for tile in range(6):
        lanes = slice(128 * tile, 128 * tile + 128)
        for k, shifted in enumerate(z_shifts(value_of(lanes), 288)):
            scratch[k, :, lanes] = shifted.astype(BF)


def skip_kernel(bounds, near, own, far, weight, out_ref, scratch):
    odd = bounds[8] == 1

    def value_of(lanes):
        group, half = divmod(lanes.start // 128, 2)
        here = slice(128 * half, 128 * half + 128)
        if group == 1:
            return own[48:336, here].astype(F32)
        first, second = near[48:336, here].astype(F32), far[48:336, here].astype(F32)
        return jnp.where(odd, first, second) if group == 0 else jnp.where(odd, second, first)

    fill_shifts(value_of, scratch)
    for g in range(2):
        out_ref[g] = closing_sum(weight, scratch, g)


def last_kernel(bounds, coarse_ref, w_coarse, wupr, weight, part_ref, out_ref, state, raw, up, scratch):
    value = coarse_ref[...].reshape(224, 512).astype(F32)
    for layer in range(4):
        rows_in = (14 - 2 * layer) * 16
        rows = rows_in - 32
        state[0, :rows_in] = value.astype(BF)
        state[1, :rows_in] = pltpu.roll(value, rows_in - 1, 0).astype(BF)
        state[2, :rows_in] = pltpu.roll(value, rows_in - 2, 0).astype(BF)
        low = jnp.zeros((rows, 256), F32)
        high = jnp.zeros((rows, 256), F32)
        zero = jnp.zeros((128, 128), BF)
        for oa in range(3):
            for ob in range(3):
                w = [w_coarse[layer, 9 * oa + 3 * ob + oz] for oz in range(3)]
                middle = jnp.concatenate(w, axis=1)
                w_low = jnp.concatenate([jnp.concatenate([w[1], w[2], zero], axis=1), middle], axis=0)
                w_high = jnp.concatenate([middle, jnp.concatenate([zero, w[0], w[1]], axis=1)], axis=0)
                low += dot(state[ob, 16 * oa : 16 * oa + rows, 0:384], w_low, NT)
                high += dot(state[ob, 16 * oa : 16 * oa + rows, 128:512], w_high, NT)
        index = iota((rows, 512), 0)
        a = (index >> 4) - 4 + layer
        b = index & 15
        kept = (a >= bounds[4]) & (a <= bounds[5]) & (b < 12 - 2 * layer)
        kept = kept & (b - 4 + layer >= bounds[6]) & (b - 4 + layer <= bounds[7])
        value = jnp.where(kept, jnp.maximum(jnp.concatenate([low, high], axis=1), 0.0), 0.0)
        value = value.astype(BF).astype(F32)
    cells = jnp.concatenate(
        [value[16 * a : 16 * a + 8, 128 * z : 128 * z + 128] for z in range(4) for a in range(6)], axis=0
    ).astype(BF)
    for i in range(0, 16, 2):
        pair = dot(cells, jnp.concatenate([wupr[i], wupr[i + 1]], axis=0), NT)
        for half in range(2):
            for z in range(4):
                for a in range(6):
                    raw[32 * (i + half) + 8 * z : 32 * (i + half) + 8 * z + 8, 128 * a : 128 * a + 128] = pair[
                        48 * z + 8 * a : 48 * z + 8 * a + 8, 128 * half : 128 * half + 128
                    ]
    from_groups = regroup(288, 512, 1, 3)
    for g in range(3):
        up[:, 256 * g : 256 * g + 256] = dot(from_groups, raw[:, 256 * g : 256 * g + 256].astype(BF), NN)
    fill_shifts(lambda lanes: up[:, lanes], scratch)
    row, column = iota((256, 256), 0), iota((256, 256), 1)
    to_channels = jnp.where(column == ((row & 7) << 5) + (row >> 3), 1.0, 0.0).astype(BF)
    for g in range(2):
        total = (closing_sum(weight, scratch, g) + part_ref[g]).astype(BF)
        out_ref[:, 8 * g : 8 * g + 8, :] = dot(to_channels, total, NN).reshape(32, 8, 256).astype(BF)


def banded(source, target, channels):
    inputs = source.shape[2]
    repeat = iota((inputs, 512), 0) - channels == iota((inputs, 512), 1) & 31
    repeat = jnp.where(repeat, 1.0, 0.0).astype(BF)
    plane = (iota((32, 512), 1) >> 5) - 3
    for t in range(9):
        tiled = dot(jnp.concatenate([source[t], source[t + 9], source[t + 18]], axis=0), repeat, NN)
        for x in range(8):
            rows = jnp.where(plane == x + 2, tiled[64:], 0.0)
            rows = jnp.where(plane == x + 1, tiled[32:64], rows)
            rows = jnp.where(plane == x, tiled[:32], rows)
            target[t, 32 * x : 32 * x + 32] = rows.astype(BF)


def by_offset(tall, target):
    for i in range(16):
        for x in range(4):
            target[i, 32 * x : 32 * x + 32] = tall[pl.ds(16 * x + i, 32, stride=64), :].astype(BF)


def prepare_first_kernel(first, down, w1, dwr, tall):
    banded(first, w1, 0)
    tall[...] = down[...].astype(F32)
    by_offset(tall, dwr)


def prepare_last_kernel(closing, up, skip_weight, up_weight, wupr, tall):
    banded(closing, skip_weight, 0)
    banded(closing, up_weight, 32)
    for k in range(16):
        tall[128 * k : 128 * k + 128] = up[:, 128 * k : 128 * k + 128].astype(F32).T
    by_offset(tall, wupr)


VMEM = pl.BlockSpec(memory_space=pltpu.VMEM)
SMEM = pl.BlockSpec(memory_space=pltpu.SMEM)


def call(body, shapes, scratch, n_in, scalars, flops, limit):
    return pl.pallas_call(
        body,
        out_shape=[jax.ShapeDtypeStruct(s, t) for s, t in shapes],
        in_specs=([SMEM] if scalars else []) + [VMEM] * n_in,
        out_specs=[VMEM] * len(shapes),
        scratch_shapes=[pltpu.VMEM(s, t) for s, t in scratch],
        compiler_params=pltpu.CompilerParams(vmem_limit_bytes=limit << 20),
        cost_estimate=pl.CostEstimate(flops=flops, bytes_accessed=4 << 20, transcendentals=0),
    )


def ones_where(condition):
    return jnp.where(condition, 1.0, 0.0).astype(BF)


def place_own():
    r, lane = iota((512, 512), 0), iota((512, 512), 1)
    return ones_where((lane & 31 == r >> 4) & (lane >> 5 == r & 15))


def swap(array, axis, start):
    pairs = [(i, i + 1) for i in range(start, lax.axis_size(axis) - 1, 2)]
    return lax.ppermute(array, axis, pairs + [(j, i) for i, j in pairs])


def y_swaps(bottom, top, odd_y):
    chips = swap(jnp.where(odd_y, top, bottom), "sy", 1)
    cores = swap(jnp.where(odd_y, bottom, top), "sy", 0)
    return chips, cores


def local(volume, w_first, down_weight, w_coarse, w_up, closing_weight):
    ix, iy = lax.axis_index("sx"), lax.axis_index("sy")
    first_x, last_x = ix == 0, ix == lax.axis_size("sx") - 1
    first_y, last_y = iy == 0, iy == lax.axis_size("sy") - 1
    bounds = jnp.stack(
        [
            jnp.where(first_x, 0, -99),
            jnp.where(last_x, 15, 99),
            jnp.where(first_y, 0, -99),
            jnp.where(last_y, 15, 99),
            jnp.where(first_x, 0, -99),
            jnp.where(last_x, 3, 99),
            jnp.where(first_y, 0, -99),
            jnp.where(last_y, 3, 99),
            ix & 1,
            iy & 1,
        ]
    ).astype(jnp.int32)
    odd = (ix & 1) == 1
    own = dot(volume.reshape(512, 256), place_own(), TN).astype(BF)
    odd_y = (iy & 1) == 1
    chips, cores = y_swaps(own[0:80], own[176:256], odd_y)
    own, to_near, to_far = call(
        pack_kernel, [((416, 512), BF), ((520, 128), BF), ((520, 128), BF)], [], 3, True, 1 << 20, 8
    )(bounds, own, chips, cores)
    near = swap(to_near, "sx", 0)
    far = swap(to_far, "sx", 1)
    w1, dwr = call(
        prepare_first_kernel, [((9, 256, 512), BF), ((16, 128, 128), BF)], [((2048, 128), F32)], 2, False, 1 << 27, 12
    )(w_first, down_weight)
    skip, cells = ((384, 256), BF), ((4, 8, 512), BF)
    skip_near, skip_own, to_far, coarse_own = call(
        near_kernel,
        [skip, skip, cells, ((2, 8, 512), BF)],
        [((3, 416, 512), BF), ((512, 512), BF)],
        4,
        True,
        2 << 30,
        24,
    )(bounds, own, near, w1, dwr)
    far_cells = swap(to_far, "sx", 1)
    skip_far, to_near = call(
        far_kernel, [skip, cells], [((3, 416, 512), BF), ((512, 256), BF)], 5, True, 1 << 30, 24
    )(bounds, own, far, w1, dwr, coarse_own)
    near_cells = swap(to_near, "sx", 0)
    skip_weight, up_weight, wupr = call(
        prepare_last_kernel,
        [((9, 256, 512), BF), ((9, 256, 512), BF), ((16, 128, 128), BF)],
        [((2048, 128), F32)],
        2,
        False,
        1 << 28,
        16,
    )(closing_weight, w_up)
    (part,) = call(skip_kernel, [((2, 256, 256), F32)], [((3, 288, 768), BF)], 4, True, 2 << 30, 16)(
        bounds, skip_near, skip_own, skip_far, skip_weight
    )
    odd_order = jnp.concatenate([near_cells, to_far[:2], to_near, far_cells], axis=0)
    even_order = jnp.concatenate([far_cells, to_near, to_far[2:], near_cells], axis=0)
    coarse = jnp.where(odd, odd_order, even_order)
    chips, cores = y_swaps(coarse[:, 2:6], coarse[:, 0:4], odd_y)
    before, after = jnp.where(odd_y, cores, chips), jnp.where(odd_y, chips, cores)
    coarse = jnp.concatenate([before, coarse[:, 0:6], after, jnp.zeros((14, 2, 512), BF)], axis=1)
    (result,) = call(
        last_kernel,
        [((32, 16, 256), BF)],
        [
            ((3, 224, 512), BF),
            ((512, 768), F32),
            ((288, 768), F32),
            ((3, 288, 768), BF),
        ],
        5,
        True,
        3 << 30,
        32,
    )(bounds, coarse, w_coarse, wupr, up_weight, part)
    return result


def solution(mesh):
    return jax.shard_map(
        local,
        mesh=mesh,
        in_specs=(P(None, "sx", "sy"), P(), P(), P(), P(), P()),
        out_specs=P(None, "sx", "sy"),
        check_vma=False,
    )
```

```python
import jax
import jax.numpy as jnp
from jax import lax
from jax.experimental import pallas as pl
from jax.experimental.pallas import tpu as pltpu
from jax.sharding import PartitionSpec as P

NZ = 16
BF = jnp.bfloat16
F32 = jnp.float32
NT = (((1,), (1,)), ((), ()))
NN = (((1,), (0,)), ((), ()))
TN = (((0,), (0,)), ((), ()))


def iota(shape, dim):
    return lax.broadcasted_iota(jnp.int32, shape, dim)


def dot(a, b, dims):
    return lax.dot_general(a, b, dims, preferred_element_type=F32)


def z_shifts(value, rows):
    z = iota(value.shape, 0) & (NZ - 1)
    before = jnp.where(z == 0, 0.0, pltpu.roll(value, 1, 0))
    after = jnp.where(z == NZ - 1, 0.0, pltpu.roll(value, rows - 1, 0))
    return before, value, after


def regroup(rows, columns, row_dim, first):
    coarse = iota((rows, columns), row_dim)
    fine = iota((rows, columns), 1 - row_dim)
    offset = coarse >> 5
    y = 4 * (coarse & 7) + (offset >> 2)
    z = 4 * ((coarse >> 3) & 3) + (offset & 3)
    return jnp.where(fine == (y - first) * NZ + z, 1.0, 0.0).astype(BF)


def moved(value, start, target):
    lane = iota(value.shape, 1)
    return jnp.where(lane >> 5 == target // 32, pltpu.roll(value, (target - start) % 128, 1), 0.0)


def packed(joined, tile, fifth_tile, start):
    fifth = joined[:, 128 * fifth_tile : 128 * fifth_tile + 128]
    blocks = [moved(fifth[104 * k : 104 * k + 104], start, 32 * k) for k in range(4)]
    return jnp.concatenate(
        [joined[:, 128 * tile : 128 * tile + 128], (blocks[0] + blocks[1]) + (blocks[2] + blocks[3])], axis=0
    )


def pack_kernel(bounds, own, chips, cores, joined_ref, to_near, to_far):
    odd, odd_y = bounds[8] == 1, bounds[9] == 1
    chip, core = chips[...].astype(F32), cores[...].astype(F32)
    joined = jnp.concatenate(
        [jnp.where(odd_y, core, chip), own[...].astype(F32), jnp.where(odd_y, chip, core)], axis=0
    )
    joined_ref[...] = joined.astype(BF)
    left, right = packed(joined, 0, 1, 0), packed(joined, 3, 2, 96)
    to_far[...] = jnp.where(odd, right, left).astype(BF)
    to_near[...] = jnp.where(odd, left, right).astype(BF)


def own_window(own):
    return [own[:, 128 * tile : 128 * tile + 128].astype(F32) for tile in range(4)]


def side_window(own, halo, halo_at_left):
    tiles = own_window(own)
    fifth = halo[416:520].astype(F32)
    at_end, at_start = (
        jnp.concatenate([moved(fifth, 32 * k, lane) for k in range(4)], axis=0)
        for lane in (96, 0)
    )
    close = halo[0:416].astype(F32)
    left, right = (at_end, close, tiles[0], tiles[1]), (tiles[2], tiles[3], close, at_start)
    return [jnp.where(halo_at_left, one, other) for one, other in zip(left, right)]


def fill_edges(before, after, rows, target):
    lane = iota((rows, 128), 1)
    both = jnp.where(lane >= 96, before, jnp.where(lane < 32, after, 0.0))
    low, middle, high = z_shifts(both, rows)
    target[:, 0:128] = (pltpu.roll(low, 32, 1) + pltpu.roll(middle, 96, 1)).astype(BF)
    target[:, 128:256] = pltpu.roll(high, 32, 1).astype(BF)


def fine_groups(windows, bounds, w1, w1_edge, dwr, skip_refs, coarse_refs, vz, edges, grouped):
    to_groups = regroup(512, 384, 0, 0)
    y = (iota((384, 256), 0) >> 4) - 4
    plane = iota((384, 256), 1) >> 5
    y_inside = (y >= bounds[2]) & (y <= bounds[3])
    for k, (tiles, first_x) in enumerate(windows):
        for half in range(2):
            for oz, shifted in enumerate(z_shifts(tiles[1 + half], 416)):
                vz[k, oz, :, 128 * half : 128 * half + 128] = shifted.astype(BF)
        fill_edges(tiles[0], tiles[3], 416, edges.at[k])
        summed = jnp.zeros((384, 256), F32)
        for oy in range(3):
            for oz in range(3):
                summed += dot(vz[k, oz, 16 * oy : 16 * oy + 384], w1[3 * oy + oz], NT)
            summed += dot(edges[k, 16 * oy : 16 * oy + 384], w1_edge[oy], NT)
        x = plane + first_x
        inside = y_inside & (x >= bounds[0]) & (x <= bounds[1])
        skip = jnp.where(inside, jnp.maximum(summed, 0.0), 0.0).astype(BF)
        skip_refs[k][...] = skip
        grouped[:, 256 * k : 256 * k + 256] = dot(to_groups, skip, NN).astype(BF)
    count = 2 * len(windows)
    coarse = jnp.zeros((32 * count, 128), F32)
    for i in range(0, 16, 2):
        pieces = []
        for a in range(count):
            lanes = slice(128 * a, 128 * a + 128)
            pieces.append(
                jnp.concatenate([grouped[32 * i : 32 * i + 32, lanes], grouped[32 * i + 32 : 32 * i + 64, lanes]], axis=1)
            )
        coarse += dot(
            jnp.concatenate(pieces, axis=0), jnp.concatenate([dwr[i], dwr[i + 1]], axis=0), NN
        )
    for a in range(count):
        for target, first_a in coarse_refs[a // 2]:
            for z in range(4):
                cell = coarse[32 * a + 8 * z : 32 * a + 8 * z + 8].astype(BF)
                target[first_a + a % 2, :, 128 * z : 128 * z + 128] = cell


def near_kernel(bounds, own, near, w1, w1_edge, dwr, skip_near, skip_own, to_far, coarse_own, vz, edges, grouped):
    odd = bounds[8] == 1
    first_near, first_own = 2 - 2 * bounds[8], 2 * bounds[8]
    windows = ((side_window(own, near, odd), jnp.where(odd, -4, 12)), (own_window(own), 4))
    coarse = ([(to_far, first_near)], [(to_far, first_own), (coarse_own, 0)])
    fine_groups(windows, bounds, w1, w1_edge, dwr, (skip_near, skip_own), coarse, vz, edges, grouped)


def far_kernel(bounds, own, far, w1, w1_edge, dwr, coarse_own, skip_far, to_near, vz, edges, grouped):
    to_near[pl.ds(2 - 2 * bounds[8], 2)] = coarse_own[...]
    even = bounds[8] == 0
    windows = ((side_window(own, far, even), jnp.where(even, -4, 12)),)
    coarse = ([(to_near, 2 * bounds[8])],)
    fine_groups(windows, bounds, w1, w1_edge, dwr, (skip_far,), coarse, vz, edges, grouped)


def fill_shifts(tile_of, middle, edges):
    for tile in range(1, 5):
        for oz, shifted in enumerate(z_shifts(tile_of(tile), 288)):
            middle[oz, :, 128 * tile - 128 : 128 * tile] = shifted.astype(BF)
    for g in range(2):
        fill_edges(tile_of(2 * g), tile_of(2 * g + 3), 288, edges.at[g])


def closing_sum(weight, weight_edge, middle, edges, g):
    summed = jnp.zeros((256, 256), F32)
    for oy in range(3):
        rows = slice(16 * oy, 16 * oy + 256)
        for oz in range(3):
            summed += dot(weight[3 * oy + oz], middle[oz, rows, 256 * g : 256 * g + 256], NT)
        summed += dot(weight_edge[oy], edges[g, rows], NT)
    return summed


def skip_kernel(bounds, near, own, far, weight, weight_edge, out_ref, middle, edges):
    odd = bounds[8] == 1

    def tile_of(tile):
        group, half = divmod(tile, 2)
        here = slice(128 * half, 128 * half + 128)
        if group == 1:
            return own[48:336, here].astype(F32)
        first, second = near[48:336, here].astype(F32), far[48:336, here].astype(F32)
        return jnp.where(odd, first, second) if group == 0 else jnp.where(odd, second, first)

    fill_shifts(tile_of, middle, edges)
    for g in range(2):
        out_ref[g] = closing_sum(weight, weight_edge, middle, edges, g)


def last_kernel(
    bounds, coarse_ref, w_coarse, wupr, weight, weight_edge, part_ref, out_ref, state, raw, up, middle_ref, edges
):
    value = coarse_ref[...].reshape(224, 512).astype(F32)
    for layer in range(4):
        rows_in = (14 - 2 * layer) * 16
        rows = rows_in - 32
        state[0, :rows_in] = value.astype(BF)
        state[1, :rows_in] = pltpu.roll(value, rows_in - 1, 0).astype(BF)
        state[2, :rows_in] = pltpu.roll(value, rows_in - 2, 0).astype(BF)
        low = jnp.zeros((rows, 256), F32)
        high = jnp.zeros((rows, 256), F32)
        zero = jnp.zeros((128, 128), BF)
        for oa in range(3):
            for ob in range(3):
                w = [w_coarse[layer, 9 * oa + 3 * ob + oz] for oz in range(3)]
                middle = jnp.concatenate(w, axis=1)
                w_low = jnp.concatenate([jnp.concatenate([w[1], w[2], zero], axis=1), middle], axis=0)
                w_high = jnp.concatenate([middle, jnp.concatenate([zero, w[0], w[1]], axis=1)], axis=0)
                low += dot(state[ob, 16 * oa : 16 * oa + rows, 0:384], w_low, NT)
                high += dot(state[ob, 16 * oa : 16 * oa + rows, 128:512], w_high, NT)
        index = iota((rows, 512), 0)
        a = (index >> 4) - 4 + layer
        b = index & 15
        kept = (a >= bounds[4]) & (a <= bounds[5]) & (b < 12 - 2 * layer)
        kept = kept & (b - 4 + layer >= bounds[6]) & (b - 4 + layer <= bounds[7])
        value = jnp.where(kept, jnp.maximum(jnp.concatenate([low, high], axis=1), 0.0), 0.0)
        value = value.astype(BF).astype(F32)
    cells = jnp.concatenate(
        [value[16 * a : 16 * a + 8, 128 * z : 128 * z + 128] for z in range(4) for a in range(6)], axis=0
    ).astype(BF)
    for i in range(0, 16, 2):
        pair = dot(cells, jnp.concatenate([wupr[i], wupr[i + 1]], axis=0), NT)
        for half in range(2):
            for z in range(4):
                for a in range(6):
                    raw[32 * (i + half) + 8 * z : 32 * (i + half) + 8 * z + 8, 128 * a : 128 * a + 128] = pair[
                        48 * z + 8 * a : 48 * z + 8 * a + 8, 128 * half : 128 * half + 128
                    ]
    from_groups = regroup(288, 512, 1, 3)
    for g in range(3):
        up[:, 256 * g : 256 * g + 256] = dot(from_groups, raw[:, 256 * g : 256 * g + 256].astype(BF), NN)
    fill_shifts(lambda tile: up[:, 128 * tile : 128 * tile + 128], middle_ref, edges)
    row, column = iota((256, 256), 0), iota((256, 256), 1)
    to_channels = jnp.where(column == ((row & 7) << 5) + (row >> 3), 1.0, 0.0).astype(BF)
    for g in range(2):
        total = (closing_sum(weight, weight_edge, middle_ref, edges, g) + part_ref[g]).astype(BF)
        out_ref[:, 8 * g : 8 * g + 8, :] = dot(to_channels, total, NN).reshape(32, 8, 256).astype(BF)


def banded(source, target, edge_target, channels):
    inputs = source.shape[2]
    repeat = iota((inputs, 256), 0) - channels == iota((inputs, 256), 1) & 31
    repeat = jnp.where(repeat, 1.0, 0.0).astype(BF)
    plane = iota((32, 256), 1) >> 5
    for oy in range(3):
        before = after = jnp.zeros((32, 256), F32)
        for oz in range(3):
            t = 3 * oy + oz
            tiled = dot(jnp.concatenate([source[t], source[t + 9], source[t + 18]], axis=0), repeat, NN)
            for x in range(8):
                rows = jnp.where(plane == x + 1, tiled[64:], 0.0)
                rows = jnp.where(plane == x, tiled[32:64], rows)
                rows = jnp.where(plane == x - 1, tiled[:32], rows)
                target[t, 32 * x : 32 * x + 32] = rows.astype(BF)
            before = jnp.where(plane == 2 * oz, tiled[:32], before)
            after = jnp.where(plane == 2 * oz + 1, tiled[64:], after)
        edge_target[oy, 0:32] = before.astype(BF)
        edge_target[oy, 32:224] = jnp.zeros((192, 256), BF)
        edge_target[oy, 224:256] = after.astype(BF)


def by_offset(tall, target):
    for i in range(16):
        for x in range(4):
            target[i, 32 * x : 32 * x + 32] = tall[pl.ds(16 * x + i, 32, stride=64), :].astype(BF)


def prepare_first_kernel(first, down, w1, w1_edge, dwr, tall):
    banded(first, w1, w1_edge, 0)
    tall[...] = down[...].astype(F32)
    by_offset(tall, dwr)


def prepare_last_kernel(closing, up, skip_weight, skip_edge, up_weight, up_edge, wupr, tall):
    banded(closing, skip_weight, skip_edge, 0)
    banded(closing, up_weight, up_edge, 32)
    for k in range(16):
        tall[128 * k : 128 * k + 128] = up[:, 128 * k : 128 * k + 128].astype(F32).T
    by_offset(tall, wupr)


VMEM = pl.BlockSpec(memory_space=pltpu.VMEM)
SMEM = pl.BlockSpec(memory_space=pltpu.SMEM)


def call(body, shapes, scratch, n_in, scalars, flops, limit):
    return pl.pallas_call(
        body,
        out_shape=[jax.ShapeDtypeStruct(s, t) for s, t in shapes],
        in_specs=([SMEM] if scalars else []) + [VMEM] * n_in,
        out_specs=[VMEM] * len(shapes),
        scratch_shapes=[pltpu.VMEM(s, t) for s, t in scratch],
        compiler_params=pltpu.CompilerParams(vmem_limit_bytes=limit << 20),
        cost_estimate=pl.CostEstimate(flops=flops, bytes_accessed=4 << 20, transcendentals=0),
    )


def ones_where(condition):
    return jnp.where(condition, 1.0, 0.0).astype(BF)


def place_own():
    r, lane = iota((512, 512), 0), iota((512, 512), 1)
    return ones_where((lane & 31 == r >> 4) & (lane >> 5 == r & 15))


def swap(array, axis, start):
    pairs = [(i, i + 1) for i in range(start, lax.axis_size(axis) - 1, 2)]
    return lax.ppermute(array, axis, pairs + [(j, i) for i, j in pairs])


def y_swaps(bottom, top, odd_y):
    chips = swap(jnp.where(odd_y, top, bottom), "sy", 1)
    cores = swap(jnp.where(odd_y, bottom, top), "sy", 0)
    return chips, cores


def local(volume, w_first, down_weight, w_coarse, w_up, closing_weight):
    ix, iy = lax.axis_index("sx"), lax.axis_index("sy")
    first_x, last_x = ix == 0, ix == lax.axis_size("sx") - 1
    first_y, last_y = iy == 0, iy == lax.axis_size("sy") - 1
    bounds = jnp.stack(
        [
            jnp.where(first_x, 0, -99),
            jnp.where(last_x, 15, 99),
            jnp.where(first_y, 0, -99),
            jnp.where(last_y, 15, 99),
            jnp.where(first_x, 0, -99),
            jnp.where(last_x, 3, 99),
            jnp.where(first_y, 0, -99),
            jnp.where(last_y, 3, 99),
            ix & 1,
            iy & 1,
        ]
    ).astype(jnp.int32)
    odd = (ix & 1) == 1
    own = dot(volume.reshape(512, 256), place_own(), TN).astype(BF)
    odd_y = (iy & 1) == 1
    chips, cores = y_swaps(own[0:80], own[176:256], odd_y)
    own, to_near, to_far = call(
        pack_kernel, [((416, 512), BF), ((520, 128), BF), ((520, 128), BF)], [], 3, True, 1 << 20, 8
    )(bounds, own, chips, cores)
    near = swap(to_near, "sx", 0)
    far = swap(to_far, "sx", 1)
    weight, edge, offsets = ((9, 256, 256), BF), ((3, 256, 256), BF), ((16, 128, 128), BF)
    w1, w1_edge, dwr = call(
        prepare_first_kernel, [weight, edge, offsets], [((2048, 128), F32)], 2, False, 1 << 27, 8
    )(w_first, down_weight)
    skip, cells = ((384, 256), BF), ((4, 8, 512), BF)
    skip_near, skip_own, to_far, coarse_own = call(
        near_kernel,
        [skip, skip, cells, ((2, 8, 512), BF)],
        [((2, 3, 416, 256), BF), ((2, 416, 256), BF), ((512, 512), BF)],
        5,
        True,
        2 << 30,
        10,
    )(bounds, own, near, w1, w1_edge, dwr)
    far_cells = swap(to_far, "sx", 1)
    skip_far, to_near = call(
        far_kernel,
        [skip, cells],
        [((1, 3, 416, 256), BF), ((1, 416, 256), BF), ((512, 256), BF)],
        6,
        True,
        1 << 30,
        10,
    )(bounds, own, far, w1, w1_edge, dwr, coarse_own)
    near_cells = swap(to_near, "sx", 0)
    skip_weight, skip_edge, up_weight, up_edge, wupr = call(
        prepare_last_kernel, [weight, edge, weight, edge, offsets], [((2048, 128), F32)], 2, False, 1 << 28, 10
    )(closing_weight, w_up)
    shifts = [((3, 288, 512), BF), ((2, 288, 256), BF)]
    (part,) = call(skip_kernel, [((2, 256, 256), F32)], shifts, 5, True, 2 << 30, 8)(
        bounds, skip_near, skip_own, skip_far, skip_weight, skip_edge
    )
    odd_order = jnp.concatenate([near_cells, to_far[:2], to_near, far_cells], axis=0)
    even_order = jnp.concatenate([far_cells, to_near, to_far[2:], near_cells], axis=0)
    coarse = jnp.where(odd, odd_order, even_order)
    chips, cores = y_swaps(coarse[:, 2:6], coarse[:, 0:4], odd_y)
    before, after = jnp.where(odd_y, cores, chips), jnp.where(odd_y, chips, cores)
    coarse = jnp.concatenate([before, coarse[:, 0:6], after, jnp.zeros((14, 2, 512), BF)], axis=1)
    (result,) = call(
        last_kernel,
        [((32, 16, 256), BF)],
        [((3, 224, 512), BF), ((512, 768), F32), ((288, 768), F32)] + shifts,
        6,
        True,
        3 << 30,
        16,
    )(bounds, coarse, w_coarse, wupr, up_weight, up_edge, part)
    return result


def solution(mesh):
    return jax.shard_map(
        local,
        mesh=mesh,
        in_specs=(P(None, "sx", "sy"), P(), P(), P(), P(), P()),
        out_specs=P(None, "sx", "sy"),
        check_vma=False,
    )
```

```python
import jax
import jax.numpy as jnp
import numpy as np
from jax import lax
from jax.experimental import pallas as pl
from jax.experimental.pallas import tpu as pltpu
from jax.sharding import PartitionSpec as P

NZ = 16
BF = jnp.bfloat16
F32 = jnp.float32
NT = (((1,), (1,)), ((), ()))
NN = (((1,), (0,)), ((), ()))
TN = (((0,), (0,)), ((), ()))


def iota(shape, dim):
    return lax.broadcasted_iota(jnp.int32, shape, dim)


def dot(a, b, dims):
    return lax.dot_general(a, b, dims, preferred_element_type=F32)


def z_shifts(value, rows):
    z = iota(value.shape, 0) & (NZ - 1)
    before = jnp.where(z == 0, 0.0, pltpu.roll(value, 1, 0))
    after = jnp.where(z == NZ - 1, 0.0, pltpu.roll(value, rows - 1, 0))
    return before, value, after


def regroup():
    coarse, fine = np.arange(512)[:, None], np.arange(384)[None]
    y = 4 * (coarse & 7) + (coarse >> 7)
    z = 4 * (coarse >> 3 & 3) + (coarse >> 5 & 3)
    return fine == y * NZ + z


def moved(value, start, target):
    lane = iota(value.shape, 1)
    return jnp.where(lane >> 5 == target // 32, pltpu.roll(value, (target - start) % 128, 1), 0.0)


def packed(joined, tile, fifth_tile, start):
    fifth = joined[:, 128 * fifth_tile : 128 * fifth_tile + 128]
    blocks = [moved(fifth[104 * k : 104 * k + 104], start, 32 * k) for k in range(4)]
    return jnp.concatenate(
        [joined[:, 128 * tile : 128 * tile + 128], (blocks[0] + blocks[1]) + (blocks[2] + blocks[3])], axis=0
    )


def pack_kernel(bounds, own, chips, cores, joined_ref, to_near, to_far):
    odd, odd_y = bounds[8] == 1, bounds[9] == 1
    chip, core = chips[...].astype(F32), cores[...].astype(F32)
    joined = jnp.concatenate(
        [jnp.where(odd_y, core, chip), own[...].astype(F32), jnp.where(odd_y, chip, core)], axis=0
    )
    joined_ref[...] = joined.astype(BF)
    left, right = packed(joined, 0, 1, 0), packed(joined, 3, 2, 96)
    to_far[...] = jnp.where(odd, right, left).astype(BF)
    to_near[...] = jnp.where(odd, left, right).astype(BF)


def own_window(own):
    return [own[:, 128 * tile : 128 * tile + 128].astype(F32) for tile in range(4)]


def side_window(own, halo, halo_at_left):
    tiles = own_window(own)
    fifth = halo[416:520].astype(F32)
    at_end, at_start = (
        jnp.concatenate([moved(fifth, 32 * k, lane) for k in range(4)], axis=0)
        for lane in (96, 0)
    )
    close = halo[0:416].astype(F32)
    left, right = (at_end, close, tiles[0], tiles[1]), (tiles[2], tiles[3], close, at_start)
    return [jnp.where(halo_at_left, one, other) for one, other in zip(left, right)]


def fill_edges(before, after, rows, target):
    lane = iota((rows, 128), 1)
    both = jnp.where(lane >= 96, before, jnp.where(lane < 32, after, 0.0))
    low, middle, high = z_shifts(both, rows)
    target[:, 0:128] = (pltpu.roll(low, 32, 1) + pltpu.roll(middle, 96, 1)).astype(BF)
    target[:, 128:256] = pltpu.roll(high, 32, 1).astype(BF)


def fine_groups(windows, bounds, to_groups, w1, w1_edge, dwr, skip_refs, coarse_refs, vz, edges, grouped):
    y = (iota((384, 256), 0) >> 4) - 4
    plane = iota((384, 256), 1) >> 5
    y_inside = (y >= bounds[2]) & (y <= bounds[3])
    for k, (tiles, first_x) in enumerate(windows):
        for half in range(2):
            for oz, shifted in enumerate(z_shifts(tiles[1 + half], 416)):
                vz[k, oz, :, 128 * half : 128 * half + 128] = shifted.astype(BF)
        fill_edges(tiles[0], tiles[3], 416, edges.at[k])
        summed = jnp.zeros((384, 256), F32)
        for oy in range(3):
            for oz in range(3):
                summed += dot(vz[k, oz, 16 * oy : 16 * oy + 384], w1[3 * oy + oz], NT)
            summed += dot(edges[k, 16 * oy : 16 * oy + 384], w1_edge[oy], NT)
        x = plane + first_x
        inside = y_inside & (x >= bounds[0]) & (x <= bounds[1])
        skip = jnp.where(inside, jnp.maximum(summed, 0.0), 0.0).astype(BF)
        skip_refs[k][...] = skip
        grouped[:, 256 * k : 256 * k + 256] = dot(to_groups[...], skip, NN).astype(BF)
    count = 2 * len(windows)
    coarse = jnp.zeros((32 * count, 128), F32)
    for i in range(0, 16, 2):
        pieces = []
        for a in range(count):
            lanes = slice(128 * a, 128 * a + 128)
            pieces.append(
                jnp.concatenate([grouped[32 * i : 32 * i + 32, lanes], grouped[32 * i + 32 : 32 * i + 64, lanes]], axis=1)
            )
        coarse += dot(
            jnp.concatenate(pieces, axis=0), jnp.concatenate([dwr[i], dwr[i + 1]], axis=0), NN
        )
    for a in range(count):
        for target, first_a in coarse_refs[a // 2]:
            for z in range(4):
                cell = coarse[32 * a + 8 * z : 32 * a + 8 * z + 8].astype(BF)
                target[first_a + a % 2, :, 128 * z : 128 * z + 128] = cell


def own_kernel(bounds, own, groups, w1, w1_edge, dwr, skip_own, coarse_own, vz, edges, grouped):
    coarse = ([(coarse_own, 0)],)
    windows = ((own_window(own), 4),)
    fine_groups(windows, bounds, groups, w1, w1_edge, dwr, (skip_own,), coarse, vz, edges, grouped)


def side_kernel(at_left, bounds, own, halo, groups, w1, w1_edge, dwr, coarse_own, skip, cells, vz, edges, grouped):
    cells[pl.ds(2 * at_left, 2)] = coarse_own[...]
    windows = ((side_window(own, halo, at_left == 1), 12 - 16 * at_left),)
    coarse = ([(cells, 2 - 2 * at_left)],)
    fine_groups(windows, bounds, groups, w1, w1_edge, dwr, (skip,), coarse, vz, edges, grouped)


def near_kernel(bounds, *refs):
    side_kernel(bounds[8], bounds, *refs)


def far_kernel(bounds, *refs):
    side_kernel(1 - bounds[8], bounds, *refs)


def fill_shifts(tile_of, middle, edges):
    for tile in range(1, 5):
        for oz, shifted in enumerate(z_shifts(tile_of(tile), 288)):
            middle[oz, :, 128 * tile - 128 : 128 * tile] = shifted.astype(BF)
    for g in range(2):
        fill_edges(tile_of(2 * g), tile_of(2 * g + 3), 288, edges.at[g])


def closing_sum(weight, weight_edge, middle, edges, g):
    summed = jnp.zeros((256, 256), F32)
    for oy in range(3):
        rows = slice(16 * oy, 16 * oy + 256)
        for oz in range(3):
            summed += dot(weight[3 * oy + oz], middle[oz, rows, 256 * g : 256 * g + 256], NT)
        summed += dot(weight_edge[oy], edges[g, rows], NT)
    return summed


def skip_kernel(bounds, near, own, far, weight, weight_edge, out_ref, middle, edges):
    odd = bounds[8] == 1

    def tile_of(tile):
        group, half = divmod(tile, 2)
        here = slice(128 * half, 128 * half + 128)
        if group == 1:
            return own[48:336, here].astype(F32)
        first, second = near[48:336, here].astype(F32), far[48:336, here].astype(F32)
        return jnp.where(odd, first, second) if group == 0 else jnp.where(odd, second, first)

    fill_shifts(tile_of, middle, edges)
    for g in range(2):
        out_ref[g] = closing_sum(weight, weight_edge, middle, edges, g)


def last_kernel(
    bounds,
    coarse_ref,
    w_coarse,
    wupr,
    from_groups,
    weight,
    weight_edge,
    part_ref,
    out_ref,
    state,
    narrow,
    raw,
    up,
    middle_ref,
    edges,
):
    value = coarse_ref[...].reshape(224, 512).astype(F32)
    for layer in range(4):
        span = 12 - 2 * layer
        width = 16 if layer < 2 else 8
        for ob in range(3):
            shifted = pltpu.roll(value, value.shape[0] - ob, 0) if ob else value
            if layer == 2:
                shifted = jnp.concatenate([shifted[16 * a : 16 * a + 8] for a in range(10)], axis=0)
            if layer < 2:
                state[ob, : 16 * (span + 2)] = shifted.astype(BF)
            else:
                narrow[ob, : 8 * (span + 2)] = shifted
        rows = span * width
        low = jnp.zeros((rows, 256), F32)
        high = jnp.zeros((rows, 256), F32)
        zero = jnp.zeros((128, 128), BF)
        for oa in range(3):
            for ob in range(3):
                w = [w_coarse[layer, 9 * oa + 3 * ob + oz] for oz in range(3)]
                middle = jnp.concatenate(w, axis=1)
                w_low = jnp.concatenate([jnp.concatenate([w[1], w[2], zero], axis=1), middle], axis=0)
                w_high = jnp.concatenate([middle, jnp.concatenate([zero, w[0], w[1]], axis=1)], axis=0)
                if layer < 2:
                    cells = state[ob, 16 * oa : 16 * oa + rows]
                else:
                    cells = narrow[ob, 8 * oa : 8 * oa + rows].astype(BF)
                low += dot(cells[:, 0:384], w_low, NT)
                high += dot(cells[:, 128:512], w_high, NT)
        index = iota((rows, 128), 0)
        a = index // width - 4 + layer
        b = index % width - 4 + layer
        kept = (a >= bounds[4]) & (a <= bounds[5]) & (b < 8 - layer)
        kept = kept & (b >= bounds[6]) & (b <= bounds[7])
        value = jnp.concatenate(
            [
                jnp.where(kept, jnp.maximum(half[:, side : side + 128], 0.0), 0.0)
                for half in (low, high)
                for side in (0, 128)
            ],
            axis=1,
        )
        value = value.astype(BF).astype(F32)
    cells = jnp.concatenate(
        [value[8 * a : 8 * a + 8, 128 * z : 128 * z + 128] for z in range(4) for a in range(6)], axis=0
    ).astype(BF)
    for i in range(0, 16, 2):
        pair = dot(cells, jnp.concatenate([wupr[i], wupr[i + 1]], axis=0), NT)
        for half in range(2):
            for z in range(4):
                for a in range(6):
                    raw[32 * (i + half) + 8 * z : 32 * (i + half) + 8 * z + 8, 128 * a : 128 * a + 128] = pair[
                        48 * z + 8 * a : 48 * z + 8 * a + 8, 128 * half : 128 * half + 128
                    ]
    for g in range(3):
        up[:, 256 * g : 256 * g + 256] = dot(from_groups[...], raw[:, 256 * g : 256 * g + 256].astype(BF), NN)
    fill_shifts(lambda tile: up[:, 128 * tile : 128 * tile + 128], middle_ref, edges)
    row, column = iota((256, 256), 0), iota((256, 256), 1)
    to_channels = jnp.where(column == ((row & 7) << 5) + (row >> 3), 1.0, 0.0).astype(BF)
    for g in range(2):
        total = (closing_sum(weight, weight_edge, middle_ref, edges, g) + part_ref[g]).astype(BF)
        out_ref[:, 8 * g : 8 * g + 8, :] = dot(to_channels, total, NN).reshape(32, 8, 256).astype(BF)


def banded(source, target, edge_target, channels):
    inputs = source.shape[2]
    repeat = iota((inputs, 256), 0) - channels == iota((inputs, 256), 1) & 31
    repeat = jnp.where(repeat, 1.0, 0.0).astype(BF)
    plane = iota((32, 256), 1) >> 5
    for oy in range(3):
        before = after = jnp.zeros((32, 256), F32)
        for oz in range(3):
            t = 3 * oy + oz
            tiled = dot(jnp.concatenate([source[t], source[t + 9], source[t + 18]], axis=0), repeat, NN)
            for x in range(8):
                rows = jnp.where(plane == x + 1, tiled[64:], 0.0)
                rows = jnp.where(plane == x, tiled[32:64], rows)
                rows = jnp.where(plane == x - 1, tiled[:32], rows)
                target[t, 32 * x : 32 * x + 32] = rows.astype(BF)
            before = jnp.where(plane == 2 * oz, tiled[:32], before)
            after = jnp.where(plane == 2 * oz + 1, tiled[64:], after)
        edge_target[oy, 0:32] = before.astype(BF)
        edge_target[oy, 32:224] = jnp.zeros((192, 256), BF)
        edge_target[oy, 224:256] = after.astype(BF)


def by_offset(tall, target):
    for i in range(16):
        for x in range(4):
            target[i, 32 * x : 32 * x + 32] = tall[pl.ds(16 * x + i, 32, stride=64), :].astype(BF)


def prepare_first_kernel(first, down, w1, w1_edge, dwr, tall):
    banded(first, w1, w1_edge, 0)
    tall[...] = down[...].astype(F32)
    by_offset(tall, dwr)


def prepare_last_kernel(closing, up, skip_weight, skip_edge, up_weight, up_edge, wupr, tall):
    banded(closing, skip_weight, skip_edge, 0)
    banded(closing, up_weight, up_edge, 32)
    for k in range(16):
        tall[128 * k : 128 * k + 128] = up[:, 128 * k : 128 * k + 128].astype(F32).T
    by_offset(tall, wupr)


VMEM = pl.BlockSpec(memory_space=pltpu.VMEM)
SMEM = pl.BlockSpec(memory_space=pltpu.SMEM)


def call(body, shapes, scratch, n_in, scalars, flops, limit):
    return pl.pallas_call(
        body,
        out_shape=[jax.ShapeDtypeStruct(s, t) for s, t in shapes],
        in_specs=([SMEM] if scalars else []) + [VMEM] * n_in,
        out_specs=[VMEM] * len(shapes),
        scratch_shapes=[pltpu.VMEM(s, t) for s, t in scratch],
        compiler_params=pltpu.CompilerParams(vmem_limit_bytes=limit << 20),
        cost_estimate=pl.CostEstimate(flops=flops, bytes_accessed=4 << 20, transcendentals=0),
    )


def ones_where(condition):
    return jnp.where(condition, 1.0, 0.0).astype(BF)


def place_own():
    r, lane = iota((512, 512), 0), iota((512, 512), 1)
    return ones_where((lane & 31 == r >> 4) & (lane >> 5 == r & 15))


def swap(array, axis, start):
    pairs = [(i, i + 1) for i in range(start, lax.axis_size(axis) - 1, 2)]
    return lax.ppermute(array, axis, pairs + [(j, i) for i, j in pairs])


def y_swaps(bottom, top, odd_y):
    chips = swap(jnp.where(odd_y, top, bottom), "sy", 1)
    cores = swap(jnp.where(odd_y, bottom, top), "sy", 0)
    return chips, cores


def local(volume, w_first, down_weight, w_coarse, w_up, closing_weight):
    ix, iy = lax.axis_index("sx"), lax.axis_index("sy")
    first_x, last_x = ix == 0, ix == lax.axis_size("sx") - 1
    first_y, last_y = iy == 0, iy == lax.axis_size("sy") - 1
    bounds = jnp.stack(
        [
            jnp.where(first_x, 0, -99),
            jnp.where(last_x, 15, 99),
            jnp.where(first_y, 0, -99),
            jnp.where(last_y, 15, 99),
            jnp.where(first_x, 0, -99),
            jnp.where(last_x, 3, 99),
            jnp.where(first_y, 0, -99),
            jnp.where(last_y, 3, 99),
            ix & 1,
            iy & 1,
        ]
    ).astype(jnp.int32)
    odd = (ix & 1) == 1
    own = dot(volume.reshape(512, 256), place_own(), TN).astype(BF)
    odd_y = (iy & 1) == 1
    chips, cores = y_swaps(own[0:80], own[176:256], odd_y)
    own, to_near, to_far = call(
        pack_kernel, [((416, 512), BF), ((520, 128), BF), ((520, 128), BF)], [], 3, True, 1 << 20, 8
    )(bounds, own, chips, cores)
    far = swap(to_far, "sx", 1)
    near = swap(to_near, "sx", 0)
    weight, edge, offsets = ((9, 256, 256), BF), ((3, 256, 256), BF), ((16, 128, 128), BF)
    w1, w1_edge, dwr = call(
        prepare_first_kernel, [weight, edge, offsets], [((2048, 128), F32)], 2, False, 1 << 27, 8
    )(w_first, down_weight)
    skip, cells = ((384, 256), BF), ((4, 8, 512), BF)
    groups = jnp.asarray(regroup(), BF)
    scratch = [((1, 3, 416, 256), BF), ((1, 416, 256), BF), ((512, 256), BF)]
    skip_own, coarse_own = call(own_kernel, [skip, ((2, 8, 512), BF)], scratch, 5, True, 1 << 30, 10)(
        bounds, own, groups, w1, w1_edge, dwr
    )
    skip_near, to_far = call(near_kernel, [skip, cells], scratch, 7, True, 1 << 30, 10)(
        bounds, own, near, groups, w1, w1_edge, dwr, coarse_own
    )
    far_cells = swap(to_far, "sx", 1)
    skip_far, to_near = call(far_kernel, [skip, cells], scratch, 7, True, 1 << 30, 10)(
        bounds, own, far, groups, w1, w1_edge, dwr, coarse_own
    )
    near_cells = swap(to_near, "sx", 0)
    skip_weight, skip_edge, up_weight, up_edge, wupr = call(
        prepare_last_kernel, [weight, edge, weight, edge, offsets], [((2048, 128), F32)], 2, False, 1 << 28, 10
    )(closing_weight, w_up)
    shifts = [((3, 288, 512), BF), ((2, 288, 256), BF)]
    (part,) = call(skip_kernel, [((2, 256, 256), F32)], shifts, 5, True, 2 << 30, 8)(
        bounds, skip_near, skip_own, skip_far, skip_weight, skip_edge
    )
    odd_order = jnp.concatenate([near_cells, to_far[:2], to_near, far_cells], axis=0)
    even_order = jnp.concatenate([far_cells, to_near, to_far[2:], near_cells], axis=0)
    coarse = jnp.where(odd, odd_order, even_order)
    chips, cores = y_swaps(coarse[:, 2:6], coarse[:, 0:4], odd_y)
    before, after = jnp.where(odd_y, cores, chips), jnp.where(odd_y, chips, cores)
    coarse = jnp.concatenate([before, coarse[:, 0:6], after, jnp.zeros((14, 2, 512), BF)], axis=1)
    (result,) = call(
        last_kernel,
        [((32, 16, 256), BF)],
        [((3, 224, 512), BF), ((3, 80, 512), F32), ((512, 768), F32), ((288, 768), F32)] + shifts,
        7,
        True,
        3 << 30,
        16,
    )(bounds, coarse, w_coarse, wupr, jnp.asarray(regroup().T[48:336], BF), up_weight, up_edge, part)
    return result


def solution(mesh):
    return jax.shard_map(
        local,
        mesh=mesh,
        in_specs=(P(None, "sx", "sy"), P(), P(), P(), P(), P()),
        out_specs=P(None, "sx", "sy"),
        check_vma=False,
    )
```

```python
import jax
import jax.numpy as jnp
import numpy as np
from jax import lax
from jax.experimental import pallas as pl
from jax.experimental.pallas import tpu as pltpu
from jax.sharding import PartitionSpec as P

NZ = 16
BF = jnp.bfloat16
F32 = jnp.float32
NT = (((1,), (1,)), ((), ()))
NN = (((1,), (0,)), ((), ()))
TN = (((0,), (0,)), ((), ()))


def iota(shape, dim):
    return lax.broadcasted_iota(jnp.int32, shape, dim)


def dot(a, b, dims):
    return lax.dot_general(a, b, dims, preferred_element_type=F32)


def z_shifts(value, rows):
    z = iota(value.shape, 0) & (NZ - 1)
    before = jnp.where(z == 0, 0.0, pltpu.roll(value, 1, 0))
    after = jnp.where(z == NZ - 1, 0.0, pltpu.roll(value, rows - 1, 0))
    return before, value, after


def regroup():
    coarse, fine = np.arange(512)[:, None], np.arange(384)[None]
    y = 4 * (coarse & 7) + (coarse >> 7)
    z = 4 * (coarse >> 3 & 3) + (coarse >> 5 & 3)
    return fine == y * NZ + z


def moved(value, start, target):
    lane = iota(value.shape, 1)
    return jnp.where(lane >> 5 == target // 32, pltpu.roll(value, (target - start) % 128, 1), 0.0)


def packed(joined, tile, fifth_tile, start):
    fifth = joined[:, 128 * fifth_tile : 128 * fifth_tile + 128]
    blocks = [moved(fifth[104 * k : 104 * k + 104], start, 32 * k) for k in range(4)]
    return jnp.concatenate(
        [joined[:, 128 * tile : 128 * tile + 128], (blocks[0] + blocks[1]) + (blocks[2] + blocks[3])], axis=0
    )


def pack_kernel(bounds, own, chips, cores, joined_ref, to_near, to_far):
    odd, odd_y = bounds[8] == 1, bounds[9] == 1
    chip, core = chips[...].astype(F32), cores[...].astype(F32)
    joined = jnp.concatenate(
        [jnp.where(odd_y, core, chip), own[...].astype(F32), jnp.where(odd_y, chip, core)], axis=0
    )
    joined_ref[...] = joined.astype(BF)
    left, right = packed(joined, 0, 1, 0), packed(joined, 3, 2, 96)
    to_far[...] = jnp.where(odd, right, left).astype(BF)
    to_near[...] = jnp.where(odd, left, right).astype(BF)


def own_window(own):
    return [own[:, 128 * tile : 128 * tile + 128].astype(F32) for tile in range(4)]


def side_window(own, halo, halo_at_left):
    tiles = own_window(own)
    fifth = halo[416:520].astype(F32)
    at_end, at_start = (
        jnp.concatenate([moved(fifth, 32 * k, lane) for k in range(4)], axis=0)
        for lane in (96, 0)
    )
    close = halo[0:416].astype(F32)
    left, right = (at_end, close, tiles[0], tiles[1]), (tiles[2], tiles[3], close, at_start)
    return [jnp.where(halo_at_left, one, other) for one, other in zip(left, right)]


def fill_edges(before, after, rows, target):
    lane = iota((rows, 128), 1)
    both = jnp.where(lane >= 96, before, jnp.where(lane < 32, after, 0.0))
    low, middle, high = z_shifts(both, rows)
    target[:, 0:128] = (pltpu.roll(low, 32, 1) + pltpu.roll(middle, 96, 1)).astype(BF)
    target[:, 128:256] = pltpu.roll(high, 32, 1).astype(BF)


def fine_groups(windows, bounds, to_groups, w1, w1_edge, dwr, skip_refs, coarse_refs, vz, edges, grouped):
    parts = 2 // len(windows)
    rows = 384 // parts
    chains = [(k, rows * part) for k in range(len(windows)) for part in range(parts)]
    for k, (tiles, _) in enumerate(windows):
        for half in range(2):
            for oz, shifted in enumerate(z_shifts(tiles[1 + half], 416)):
                vz[k, oz, :, 128 * half : 128 * half + 128] = shifted.astype(BF)
        fill_edges(tiles[0], tiles[3], 416, edges.at[k])
    summed = [jnp.zeros((rows, 256), F32) for _ in chains]
    for oy in range(3):
        for oz in range(4):
            for c, (k, start) in enumerate(chains):
                here = slice(start + 16 * oy, start + 16 * oy + rows)
                if oz < 3:
                    summed[c] += dot(vz[k, oz, here], w1[3 * oy + oz], NT)
                else:
                    summed[c] += dot(edges[k, here], w1_edge[oy], NT)
    for c, (k, start) in enumerate(chains):
        y = ((iota((rows, 256), 0) + start) >> 4) - 4
        x = (iota((rows, 256), 1) >> 5) + windows[k][1]
        inside = (y >= bounds[2]) & (y <= bounds[3]) & (x >= bounds[0]) & (x <= bounds[1])
        skip_refs[k][start : start + rows] = jnp.where(inside, jnp.maximum(summed[c], 0.0), 0.0).astype(BF)
    for k in range(len(windows)):
        grouped[:, 256 * k : 256 * k + 256] = dot(to_groups[...], skip_refs[k][...], NN).astype(BF)
    count = 2 * len(windows)
    coarse = jnp.zeros((32 * count, 128), F32)
    for i in range(0, 16, 2):
        pieces = []
        for a in range(count):
            lanes = slice(128 * a, 128 * a + 128)
            pieces.append(
                jnp.concatenate([grouped[32 * i : 32 * i + 32, lanes], grouped[32 * i + 32 : 32 * i + 64, lanes]], axis=1)
            )
        coarse += dot(
            jnp.concatenate(pieces, axis=0), jnp.concatenate([dwr[i], dwr[i + 1]], axis=0), NN
        )
    for a in range(count):
        for target, first_a in coarse_refs[a // 2]:
            for z in range(4):
                cell = coarse[32 * a + 8 * z : 32 * a + 8 * z + 8].astype(BF)
                target[first_a + a % 2, :, 128 * z : 128 * z + 128] = cell


def near_kernel(bounds, own, near, groups, w1, w1_edge, dwr, skip_near, skip_own, to_far, coarse_own, vz, edges, grouped):
    odd = bounds[8] == 1
    first_near, first_own = 2 - 2 * bounds[8], 2 * bounds[8]
    windows = ((side_window(own, near, odd), jnp.where(odd, -4, 12)), (own_window(own), 4))
    coarse = ([(to_far, first_near)], [(to_far, first_own), (coarse_own, 0)])
    fine_groups(windows, bounds, groups, w1, w1_edge, dwr, (skip_near, skip_own), coarse, vz, edges, grouped)


def far_kernel(bounds, own, far, groups, w1, w1_edge, dwr, coarse_own, skip_far, to_near, vz, edges, grouped):
    to_near[pl.ds(2 - 2 * bounds[8], 2)] = coarse_own[...]
    even = bounds[8] == 0
    windows = ((side_window(own, far, even), jnp.where(even, -4, 12)),)
    coarse = ([(to_near, 2 * bounds[8])],)
    fine_groups(windows, bounds, groups, w1, w1_edge, dwr, (skip_far,), coarse, vz, edges, grouped)


def fill_shifts(tile_of, middle, edges):
    for tile in range(1, 5):
        for oz, shifted in enumerate(z_shifts(tile_of(tile), 288)):
            middle[oz, :, 128 * tile - 128 : 128 * tile] = shifted.astype(BF)
    for g in range(2):
        fill_edges(tile_of(2 * g), tile_of(2 * g + 3), 288, edges.at[g])


def closing_sums(weight, weight_edge, middle, edges):
    summed = [jnp.zeros((256, 256), F32) for _ in range(2)]
    for oy in range(3):
        rows = slice(16 * oy, 16 * oy + 256)
        for oz in range(4):
            for g in range(2):
                if oz < 3:
                    summed[g] += dot(middle[oz, rows, 256 * g : 256 * g + 256], weight[3 * oy + oz], NT)
                else:
                    summed[g] += dot(edges[g, rows], weight_edge[oy], NT)
    return summed


def skip_kernel(bounds, near, own, far, weight, weight_edge, out_ref, middle, edges):
    odd = bounds[8] == 1

    def tile_of(tile):
        group, half = divmod(tile, 2)
        here = slice(128 * half, 128 * half + 128)
        if group == 1:
            return own[48:336, here].astype(F32)
        first, second = near[48:336, here].astype(F32), far[48:336, here].astype(F32)
        return jnp.where(odd, first, second) if group == 0 else jnp.where(odd, second, first)

    fill_shifts(tile_of, middle, edges)
    for g, summed in enumerate(closing_sums(weight, weight_edge, middle, edges)):
        out_ref[g] = summed


def coarse_kernel(bounds, coarse_ref, w_coarse, wupr, from_groups, up, state, raw):
    value = coarse_ref[...].reshape(224, 512).astype(F32)
    for layer in range(4):
        rows_in = (14 - 2 * layer) * 16
        rows = rows_in - 32
        state[0, :rows_in] = value.astype(BF)
        state[1, :rows_in] = pltpu.roll(value, rows_in - 1, 0).astype(BF)
        state[2, :rows_in] = pltpu.roll(value, rows_in - 2, 0).astype(BF)
        low = jnp.zeros((rows, 256), F32)
        high = jnp.zeros((rows, 256), F32)
        zero = jnp.zeros((128, 128), BF)
        for oa in range(3):
            for ob in range(3):
                w = [w_coarse[layer, 9 * oa + 3 * ob + oz] for oz in range(3)]
                middle = jnp.concatenate(w, axis=1)
                w_low = jnp.concatenate([jnp.concatenate([w[1], w[2], zero], axis=1), middle], axis=0)
                w_high = jnp.concatenate([middle, jnp.concatenate([zero, w[0], w[1]], axis=1)], axis=0)
                low += dot(state[ob, 16 * oa : 16 * oa + rows, 0:384], w_low, NT)
                high += dot(state[ob, 16 * oa : 16 * oa + rows, 128:512], w_high, NT)
        index = iota((rows, 128), 0)
        a = (index >> 4) - 4 + layer
        b = (index & 15) - 4 + layer
        kept = (a >= bounds[4]) & (a <= bounds[5]) & (b < 8 - layer) & (b >= bounds[6]) & (b <= bounds[7])
        value = jnp.concatenate(
            [
                jnp.where(kept, jnp.maximum(half[:, side : side + 128], 0.0), 0.0)
                for half in (low, high)
                for side in (0, 128)
            ],
            axis=1,
        )
        value = value.astype(BF).astype(F32)
    cells = jnp.concatenate(
        [value[16 * a : 16 * a + 8, 128 * z : 128 * z + 128] for z in range(4) for a in range(6)], axis=0
    ).astype(BF)
    for i in range(0, 16, 2):
        pair = dot(cells, jnp.concatenate([wupr[i], wupr[i + 1]], axis=0), NT)
        for half in range(2):
            for z in range(4):
                for a in range(6):
                    raw[32 * (i + half) + 8 * z : 32 * (i + half) + 8 * z + 8, 128 * a : 128 * a + 128] = pair[
                        48 * z + 8 * a : 48 * z + 8 * a + 8, 128 * half : 128 * half + 128
                    ]
    for g in range(3):
        lanes = slice(256 * g, 256 * g + 256)
        up[:, lanes] = dot(from_groups[...], raw[:, lanes].astype(BF), NN).astype(BF)


def last_kernel(up, weight, weight_edge, part_ref, out_ref, middle, edges):
    fill_shifts(lambda tile: up[:, 128 * tile : 128 * tile + 128].astype(F32), middle, edges)
    row, column = iota((256, 256), 0), iota((256, 256), 1)
    to_channels = jnp.where(column == ((row & 7) << 5) + (row >> 3), 1.0, 0.0).astype(BF)
    for g, summed in enumerate(closing_sums(weight, weight_edge, middle, edges)):
        total = (summed + part_ref[g]).astype(BF)
        out_ref[:, 8 * g : 8 * g + 8, :] = dot(to_channels, total, NT).reshape(32, 8, 256).astype(BF)


def banded(source, target, edge_target, channels):
    inputs = source.shape[2]
    repeat = iota((inputs, 256), 0) - channels == iota((inputs, 256), 1) & 31
    repeat = jnp.where(repeat, 1.0, 0.0).astype(BF)
    plane = iota((32, 256), 1) >> 5
    for oy in range(3):
        before = after = jnp.zeros((32, 256), F32)
        for oz in range(3):
            t = 3 * oy + oz
            tiled = dot(jnp.concatenate([source[t], source[t + 9], source[t + 18]], axis=0), repeat, NN)
            for x in range(8):
                rows = jnp.where(plane == x + 1, tiled[64:], 0.0)
                rows = jnp.where(plane == x, tiled[32:64], rows)
                rows = jnp.where(plane == x - 1, tiled[:32], rows)
                target[t, 32 * x : 32 * x + 32] = rows.astype(BF)
            before = jnp.where(plane == 2 * oz, tiled[:32], before)
            after = jnp.where(plane == 2 * oz + 1, tiled[64:], after)
        edge_target[oy, 0:32] = before.astype(BF)
        edge_target[oy, 32:224] = jnp.zeros((192, 256), BF)
        edge_target[oy, 224:256] = after.astype(BF)


def by_offset(tall, target):
    for i in range(16):
        for x in range(4):
            target[i, 32 * x : 32 * x + 32] = tall[pl.ds(16 * x + i, 32, stride=64), :].astype(BF)


def prepare_first_kernel(first, down, w1, w1_edge, dwr, tall):
    banded(first, w1, w1_edge, 0)
    tall[...] = down[...].astype(F32)
    by_offset(tall, dwr)


def prepare_last_kernel(closing, up, skip_weight, skip_edge, up_weight, up_edge, wupr, tall):
    banded(closing, skip_weight, skip_edge, 0)
    banded(closing, up_weight, up_edge, 32)
    for k in range(16):
        tall[128 * k : 128 * k + 128] = up[:, 128 * k : 128 * k + 128].astype(F32).T
    by_offset(tall, wupr)


VMEM = pl.BlockSpec(memory_space=pltpu.VMEM)
SMEM = pl.BlockSpec(memory_space=pltpu.SMEM)


def call(body, shapes, scratch, n_in, scalars, flops, limit):
    return pl.pallas_call(
        body,
        out_shape=[jax.ShapeDtypeStruct(s, t) for s, t in shapes],
        in_specs=([SMEM] if scalars else []) + [VMEM] * n_in,
        out_specs=[VMEM] * len(shapes),
        scratch_shapes=[pltpu.VMEM(s, t) for s, t in scratch],
        compiler_params=pltpu.CompilerParams(vmem_limit_bytes=limit << 20),
        cost_estimate=pl.CostEstimate(flops=flops, bytes_accessed=4 << 20, transcendentals=0),
    )


def ones_where(condition):
    return jnp.where(condition, 1.0, 0.0).astype(BF)


def place_own():
    r, lane = iota((512, 512), 0), iota((512, 512), 1)
    return ones_where((lane & 31 == r >> 4) & (lane >> 5 == r & 15))


def swap(array, axis, start):
    pairs = [(i, i + 1) for i in range(start, lax.axis_size(axis) - 1, 2)]
    return lax.ppermute(array, axis, pairs + [(j, i) for i, j in pairs])


def y_swaps(bottom, top, odd_y):
    chips = swap(jnp.where(odd_y, top, bottom), "sy", 1)
    cores = swap(jnp.where(odd_y, bottom, top), "sy", 0)
    return chips, cores


def local(volume, w_first, down_weight, w_coarse, w_up, closing_weight):
    ix, iy = lax.axis_index("sx"), lax.axis_index("sy")
    first_x, last_x = ix == 0, ix == lax.axis_size("sx") - 1
    first_y, last_y = iy == 0, iy == lax.axis_size("sy") - 1
    bounds = jnp.stack(
        [
            jnp.where(first_x, 0, -99),
            jnp.where(last_x, 15, 99),
            jnp.where(first_y, 0, -99),
            jnp.where(last_y, 15, 99),
            jnp.where(first_x, 0, -99),
            jnp.where(last_x, 3, 99),
            jnp.where(first_y, 0, -99),
            jnp.where(last_y, 3, 99),
            ix & 1,
            iy & 1,
        ]
    ).astype(jnp.int32)
    odd = (ix & 1) == 1
    own = dot(volume.reshape(512, 256), place_own(), TN).astype(BF)
    odd_y = (iy & 1) == 1
    chips, cores = y_swaps(own[0:80], own[176:256], odd_y)
    own, to_near, to_far = call(
        pack_kernel, [((416, 512), BF), ((520, 128), BF), ((520, 128), BF)], [], 3, True, 1 << 20, 8
    )(bounds, own, chips, cores)
    near = swap(to_near, "sx", 0)
    far = swap(to_far, "sx", 1)
    weight, edge, offsets = ((9, 256, 256), BF), ((3, 256, 256), BF), ((16, 128, 128), BF)
    w1, w1_edge, dwr = call(
        prepare_first_kernel, [weight, edge, offsets], [((2048, 128), F32)], 2, False, 1 << 27, 8
    )(w_first, down_weight)
    skip, cells = ((384, 256), BF), ((4, 8, 512), BF)
    groups = jnp.asarray(regroup(), BF)
    skip_near, skip_own, to_far, coarse_own = call(
        near_kernel,
        [skip, skip, cells, ((2, 8, 512), BF)],
        [((2, 3, 416, 256), BF), ((2, 416, 256), BF), ((512, 512), BF)],
        6,
        True,
        2 << 30,
        10,
    )(bounds, own, near, groups, w1, w1_edge, dwr)
    far_cells = swap(to_far, "sx", 1)
    skip_far, to_near = call(
        far_kernel,
        [skip, cells],
        [((1, 3, 416, 256), BF), ((1, 416, 256), BF), ((512, 256), BF)],
        7,
        True,
        1 << 30,
        10,
    )(bounds, own, far, groups, w1, w1_edge, dwr, coarse_own)
    near_cells = swap(to_near, "sx", 0)
    skip_weight, skip_edge, up_weight, up_edge, wupr = call(
        prepare_last_kernel, [weight, edge, weight, edge, offsets], [((2048, 128), F32)], 2, False, 1 << 28, 10
    )(closing_weight, w_up)
    shifts = [((3, 288, 512), BF), ((2, 288, 256), BF)]
    (part,) = call(skip_kernel, [((2, 256, 256), F32)], shifts, 5, True, 2 << 30, 8)(
        bounds, skip_near, skip_own, skip_far, skip_weight, skip_edge
    )
    odd_order = jnp.concatenate([near_cells, to_far[:2], to_near, far_cells], axis=0)
    even_order = jnp.concatenate([far_cells, to_near, to_far[2:], near_cells], axis=0)
    coarse = jnp.where(odd, odd_order, even_order)
    chips, cores = y_swaps(coarse[:, 2:6], coarse[:, 0:4], odd_y)
    before, after = jnp.where(odd_y, cores, chips), jnp.where(odd_y, chips, cores)
    coarse = jnp.concatenate([before, coarse[:, 0:6], after, jnp.zeros((14, 2, 512), BF)], axis=1)
    (up,) = call(
        coarse_kernel, [((288, 768), BF)], [((3, 224, 512), BF), ((512, 768), F32)], 4, True, 3 << 30, 12
    )(bounds, coarse, w_coarse, wupr, jnp.asarray(regroup().T[48:336], BF))
    (result,) = call(last_kernel, [((32, 16, 256), BF)], shifts, 4, False, 2 << 30, 12)(up, up_weight, up_edge, part)
    return result


def solution(mesh):
    return jax.shard_map(
        local,
        mesh=mesh,
        in_specs=(P(None, "sx", "sy"), P(), P(), P(), P(), P()),
        out_specs=P(None, "sx", "sy"),
        check_vma=False,
    )
```

```python
import jax
import jax.numpy as jnp
import numpy as np
from jax import lax
from jax.experimental import pallas as pl
from jax.experimental.pallas import tpu as pltpu
from jax.sharding import PartitionSpec as P

NZ = 16
BF = jnp.bfloat16
F32 = jnp.float32
NT = (((1,), (1,)), ((), ()))
NN = (((1,), (0,)), ((), ()))
TN = (((0,), (0,)), ((), ()))


def iota(shape, dim):
    return lax.broadcasted_iota(jnp.int32, shape, dim)


def dot(a, b, dims):
    return lax.dot_general(a, b, dims, preferred_element_type=F32)


def z_shifts(value, rows):
    z = iota(value.shape, 0) & (NZ - 1)
    before = jnp.where(z == 0, 0.0, pltpu.roll(value, 1, 0))
    after = jnp.where(z == NZ - 1, 0.0, pltpu.roll(value, rows - 1, 0))
    return before, value, after


def regroup():
    coarse, fine = np.arange(512)[:, None], np.arange(384)[None]
    y = 4 * (coarse & 7) + (coarse >> 7)
    z = 4 * (coarse >> 3 & 3) + (coarse >> 5 & 3)
    return fine == y * NZ + z


def moved(value, start, target):
    lane = iota(value.shape, 1)
    return jnp.where(lane >> 5 == target // 32, pltpu.roll(value, (target - start) % 128, 1), 0.0)


def packed(joined, tile, fifth_tile, start):
    fifth = joined[:, 128 * fifth_tile : 128 * fifth_tile + 128]
    blocks = [moved(fifth[104 * k : 104 * k + 104], start, 32 * k) for k in range(4)]
    return jnp.concatenate(
        [joined[:, 128 * tile : 128 * tile + 128], (blocks[0] + blocks[1]) + (blocks[2] + blocks[3])], axis=0
    )


def pack_kernel(bounds, own, chips, cores, joined_ref, to_near, to_far):
    odd, odd_y = bounds[8] == 1, bounds[9] == 1
    chip, core = chips[...].astype(F32), cores[...].astype(F32)
    joined = jnp.concatenate(
        [jnp.where(odd_y, core, chip), own[...].astype(F32), jnp.where(odd_y, chip, core)], axis=0
    )
    joined_ref[...] = joined.astype(BF)
    left, right = packed(joined, 0, 1, 0), packed(joined, 3, 2, 96)
    to_far[...] = jnp.where(odd, right, left).astype(BF)
    to_near[...] = jnp.where(odd, left, right).astype(BF)


def own_window(own):
    return [own[:, 128 * tile : 128 * tile + 128].astype(F32) for tile in range(4)]


def side_window(own, halo, halo_at_left):
    tiles = own_window(own)
    fifth = halo[416:520].astype(F32)
    at_end, at_start = (
        jnp.concatenate([moved(fifth, 32 * k, lane) for k in range(4)], axis=0)
        for lane in (96, 0)
    )
    close = halo[0:416].astype(F32)
    left, right = (at_end, close, tiles[0], tiles[1]), (tiles[2], tiles[3], close, at_start)
    return [jnp.where(halo_at_left, one, other) for one, other in zip(left, right)]


def fill_edges(before, after, rows, target):
    lane = iota((rows, 128), 1)
    both = jnp.where(lane >= 96, before, jnp.where(lane < 32, after, 0.0))
    low, middle, high = z_shifts(both, rows)
    target[:, 0:128] = (pltpu.roll(low, 32, 1) + pltpu.roll(middle, 96, 1)).astype(BF)
    target[:, 128:256] = pltpu.roll(high, 32, 1).astype(BF)


def fine_groups(windows, bounds, to_groups, w1, w1_edge, dwr, skip_refs, coarse_refs, vz, edges, grouped):
    parts = 2 // len(windows)
    rows = 384 // parts
    chains = [(k, rows * part) for k in range(len(windows)) for part in range(parts)]
    for k, (tiles, _) in enumerate(windows):
        for half in range(2):
            for oz, shifted in enumerate(z_shifts(tiles[1 + half], 416)):
                vz[k, oz, :, 128 * half : 128 * half + 128] = shifted.astype(BF)
        fill_edges(tiles[0], tiles[3], 416, edges.at[k])
    summed = [jnp.zeros((rows, 256), F32) for _ in chains]
    for oy in range(3):
        for oz in range(4):
            for c, (k, start) in enumerate(chains):
                here = slice(start + 16 * oy, start + 16 * oy + rows)
                if oz < 3:
                    summed[c] += dot(vz[k, oz, here], w1[3 * oy + oz], NT)
                else:
                    summed[c] += dot(edges[k, here], w1_edge[oy], NT)
    for c, (k, start) in enumerate(chains):
        y = ((iota((rows, 256), 0) + start) >> 4) - 4
        x = (iota((rows, 256), 1) >> 5) + windows[k][1]
        inside = (y >= bounds[2]) & (y <= bounds[3]) & (x >= bounds[0]) & (x <= bounds[1])
        skip_refs[k][start : start + rows] = jnp.where(inside, jnp.maximum(summed[c], 0.0), 0.0).astype(BF)
    for k in range(len(windows)):
        grouped[:, 256 * k : 256 * k + 256] = dot(to_groups[...], skip_refs[k][...], NN).astype(BF)
    count = 2 * len(windows)
    coarse = jnp.zeros((32 * count, 128), F32)
    for i in range(0, 16, 2):
        pieces = []
        for a in range(count):
            lanes = slice(128 * a, 128 * a + 128)
            pieces.append(
                jnp.concatenate([grouped[32 * i : 32 * i + 32, lanes], grouped[32 * i + 32 : 32 * i + 64, lanes]], axis=1)
            )
        coarse += dot(
            jnp.concatenate(pieces, axis=0), jnp.concatenate([dwr[i], dwr[i + 1]], axis=0), NN
        )
    for a in range(count):
        for target, first_a in coarse_refs[a // 2]:
            for z in range(4):
                cell = coarse[32 * a + 8 * z : 32 * a + 8 * z + 8].astype(BF)
                target[first_a + a % 2, :, 128 * z : 128 * z + 128] = cell


def near_kernel(bounds, own, near, groups, w1, w1_edge, dwr, skip_near, skip_own, to_far, coarse_own, vz, edges, grouped):
    odd = bounds[8] == 1
    first_near, first_own = 2 - 2 * bounds[8], 2 * bounds[8]
    windows = ((side_window(own, near, odd), jnp.where(odd, -4, 12)), (own_window(own), 4))
    coarse = ([(to_far, first_near)], [(to_far, first_own), (coarse_own, 0)])
    fine_groups(windows, bounds, groups, w1, w1_edge, dwr, (skip_near, skip_own), coarse, vz, edges, grouped)


def far_kernel(bounds, own, far, groups, w1, w1_edge, dwr, coarse_own, skip_far, to_near, vz, edges, grouped):
    to_near[pl.ds(2 - 2 * bounds[8], 2)] = coarse_own[...]
    even = bounds[8] == 0
    windows = ((side_window(own, far, even), jnp.where(even, -4, 12)),)
    coarse = ([(to_near, 2 * bounds[8])],)
    fine_groups(windows, bounds, groups, w1, w1_edge, dwr, (skip_far,), coarse, vz, edges, grouped)


def fill_shifts(tile_of, middle, edges):
    for tile in range(1, 5):
        for oz, shifted in enumerate(z_shifts(tile_of(tile), 288)):
            middle[oz, :, 128 * tile - 128 : 128 * tile] = shifted.astype(BF)
    for g in range(2):
        fill_edges(tile_of(2 * g), tile_of(2 * g + 3), 288, edges.at[g])


def closing_sums(weight, weight_edge, middle, edges):
    summed = [jnp.zeros((256, 256), F32) for _ in range(2)]
    for oy in range(3):
        rows = slice(16 * oy, 16 * oy + 256)
        for oz in range(4):
            for g in range(2):
                if oz < 3:
                    summed[g] += dot(middle[oz, rows, 256 * g : 256 * g + 256], weight[3 * oy + oz], NT)
                else:
                    summed[g] += dot(edges[g, rows], weight_edge[oy], NT)
    return summed


def skip_kernel(bounds, near, own, far, weight, weight_edge, out_ref, middle, edges):
    odd = bounds[8] == 1

    def tile_of(tile):
        group, half = divmod(tile, 2)
        here = slice(128 * half, 128 * half + 128)
        if group == 1:
            return own[48:336, here].astype(F32)
        first, second = near[48:336, here].astype(F32), far[48:336, here].astype(F32)
        return jnp.where(odd, first, second) if group == 0 else jnp.where(odd, second, first)

    fill_shifts(tile_of, middle, edges)
    for g, summed in enumerate(closing_sums(weight, weight_edge, middle, edges)):
        out_ref[g] = summed


def transpose_kernel(source, target):
    identity = jnp.where(iota((128, 128), 0) == iota((128, 128), 1), 1.0, 0.0).astype(BF)
    for t in range(0, source.shape[0], 4):
        pair = dot(identity, jnp.concatenate([source[t], source[t + 1]], axis=0), NT).astype(BF)
        target[t], target[t + 1] = pair[:, :128], pair[:, 128:]
        target[t + 2], target[t + 3] = source[t + 2].T, source[t + 3].T


def coarse_kernel(bounds, coarse_ref, w_coarse, wupr, from_groups, up, state, raw):
    value = coarse_ref[...].reshape(224, 512).astype(F32)
    for layer in range(4):
        rows_in = (14 - 2 * layer) * 16
        rows = rows_in - 32
        state[0, :rows_in] = value.astype(BF)
        state[1, :rows_in] = pltpu.roll(value, rows_in - 1, 0).astype(BF)
        state[2, :rows_in] = pltpu.roll(value, rows_in - 2, 0).astype(BF)
        low = jnp.zeros((rows, 256), F32)
        high = jnp.zeros((rows, 256), F32)
        zero = jnp.zeros((128, 128), BF)
        for oa in range(3):
            for ob in range(3):
                w = [w_coarse[27 * layer + 9 * oa + 3 * ob + oz] for oz in range(3)]
                one, two = jnp.concatenate([w[1], w[0]], axis=1), jnp.concatenate([w[2], w[1]], axis=1)
                w_low = jnp.concatenate([one, two, jnp.concatenate([zero, w[2]], axis=1)], axis=0)
                w_high = jnp.concatenate([jnp.concatenate([w[0], zero], axis=1), one, two], axis=0)
                low += dot(state[ob, 16 * oa : 16 * oa + rows, 0:384], w_low, NN)
                high += dot(state[ob, 16 * oa : 16 * oa + rows, 128:512], w_high, NN)
        index = iota((rows, 128), 0)
        a = (index >> 4) - 4 + layer
        b = (index & 15) - 4 + layer
        kept = (a >= bounds[4]) & (a <= bounds[5]) & (b < 8 - layer) & (b >= bounds[6]) & (b <= bounds[7])
        value = jnp.concatenate(
            [
                jnp.where(kept, jnp.maximum(half[:, side : side + 128], 0.0), 0.0)
                for half in (low, high)
                for side in (0, 128)
            ],
            axis=1,
        )
        value = value.astype(BF).astype(F32)
    cells = jnp.concatenate(
        [value[16 * a : 16 * a + 8, 128 * z : 128 * z + 128] for z in range(4) for a in range(6)], axis=0
    ).astype(BF)
    for i in range(0, 16, 2):
        pair = dot(cells, jnp.concatenate([wupr[i], wupr[i + 1]], axis=0), NT)
        for half in range(2):
            for z in range(4):
                for a in range(6):
                    raw[32 * (i + half) + 8 * z : 32 * (i + half) + 8 * z + 8, 128 * a : 128 * a + 128] = pair[
                        48 * z + 8 * a : 48 * z + 8 * a + 8, 128 * half : 128 * half + 128
                    ]
    for g in range(3):
        lanes = slice(256 * g, 256 * g + 256)
        up[:, lanes] = dot(from_groups[...], raw[:, lanes].astype(BF), NN).astype(BF)


def last_kernel(up, weight, weight_edge, part_ref, out_ref, middle, edges):
    fill_shifts(lambda tile: up[:, 128 * tile : 128 * tile + 128].astype(F32), middle, edges)
    row, column = iota((256, 256), 0), iota((256, 256), 1)
    to_channels = jnp.where(column == ((row & 7) << 5) + (row >> 3), 1.0, 0.0).astype(BF)
    for g, summed in enumerate(closing_sums(weight, weight_edge, middle, edges)):
        total = (summed + part_ref[g]).astype(BF)
        out_ref[:, 8 * g : 8 * g + 8, :] = dot(to_channels, total, NT).reshape(32, 8, 256).astype(BF)


def banded(source, target, edge_target, channels):
    inputs = source.shape[2]
    repeat = iota((inputs, 256), 0) - channels == iota((inputs, 256), 1) & 31
    repeat = jnp.where(repeat, 1.0, 0.0).astype(BF)
    plane = iota((32, 256), 1) >> 5
    for oy in range(3):
        before = after = jnp.zeros((32, 256), F32)
        for oz in range(3):
            t = 3 * oy + oz
            tiled = dot(jnp.concatenate([source[t], source[t + 9], source[t + 18]], axis=0), repeat, NN)
            for x in range(8):
                rows = jnp.where(plane == x + 1, tiled[64:], 0.0)
                rows = jnp.where(plane == x, tiled[32:64], rows)
                rows = jnp.where(plane == x - 1, tiled[:32], rows)
                target[t, 32 * x : 32 * x + 32] = rows.astype(BF)
            before = jnp.where(plane == 2 * oz, tiled[:32], before)
            after = jnp.where(plane == 2 * oz + 1, tiled[64:], after)
        edge_target[oy, 0:32] = before.astype(BF)
        edge_target[oy, 32:224] = jnp.zeros((192, 256), BF)
        edge_target[oy, 224:256] = after.astype(BF)


def by_offset(tall, target):
    for i in range(16):
        for x in range(4):
            target[i, 32 * x : 32 * x + 32] = tall[pl.ds(16 * x + i, 32, stride=64), :].astype(BF)


def prepare_first_kernel(first, down, w1, w1_edge, dwr, tall):
    banded(first, w1, w1_edge, 0)
    tall[...] = down[...].astype(F32)
    by_offset(tall, dwr)


def prepare_last_kernel(closing, up, skip_weight, skip_edge, up_weight, up_edge, wupr, tall):
    banded(closing, skip_weight, skip_edge, 0)
    banded(closing, up_weight, up_edge, 32)
    for k in range(16):
        tall[128 * k : 128 * k + 128] = up[:, 128 * k : 128 * k + 128].astype(F32).T
    by_offset(tall, wupr)


VMEM = pl.BlockSpec(memory_space=pltpu.VMEM)
SMEM = pl.BlockSpec(memory_space=pltpu.SMEM)


def call(body, shapes, scratch, n_in, scalars, flops, limit):
    return pl.pallas_call(
        body,
        out_shape=[jax.ShapeDtypeStruct(s, t) for s, t in shapes],
        in_specs=([SMEM] if scalars else []) + [VMEM] * n_in,
        out_specs=[VMEM] * len(shapes),
        scratch_shapes=[pltpu.VMEM(s, t) for s, t in scratch],
        compiler_params=pltpu.CompilerParams(vmem_limit_bytes=limit << 20),
        cost_estimate=pl.CostEstimate(flops=flops, bytes_accessed=4 << 20, transcendentals=0),
    )


def ones_where(condition):
    return jnp.where(condition, 1.0, 0.0).astype(BF)


def place_own():
    r, lane = iota((512, 512), 0), iota((512, 512), 1)
    return ones_where((lane & 31 == r >> 4) & (lane >> 5 == r & 15))


def swap(array, axis, start):
    pairs = [(i, i + 1) for i in range(start, lax.axis_size(axis) - 1, 2)]
    return lax.ppermute(array, axis, pairs + [(j, i) for i, j in pairs])


def y_swaps(bottom, top, odd_y):
    chips = swap(jnp.where(odd_y, top, bottom), "sy", 1)
    cores = swap(jnp.where(odd_y, bottom, top), "sy", 0)
    return chips, cores


def local(volume, w_first, down_weight, w_coarse, w_up, closing_weight):
    ix, iy = lax.axis_index("sx"), lax.axis_index("sy")
    first_x, last_x = ix == 0, ix == lax.axis_size("sx") - 1
    first_y, last_y = iy == 0, iy == lax.axis_size("sy") - 1
    bounds = jnp.stack(
        [
            jnp.where(first_x, 0, -99),
            jnp.where(last_x, 15, 99),
            jnp.where(first_y, 0, -99),
            jnp.where(last_y, 15, 99),
            jnp.where(first_x, 0, -99),
            jnp.where(last_x, 3, 99),
            jnp.where(first_y, 0, -99),
            jnp.where(last_y, 3, 99),
            ix & 1,
            iy & 1,
        ]
    ).astype(jnp.int32)
    odd = (ix & 1) == 1
    own = dot(volume.reshape(512, 256), place_own(), TN).astype(BF)
    odd_y = (iy & 1) == 1
    chips, cores = y_swaps(own[0:80], own[176:256], odd_y)
    own, to_near, to_far = call(
        pack_kernel, [((416, 512), BF), ((520, 128), BF), ((520, 128), BF)], [], 3, True, 1 << 20, 8
    )(bounds, own, chips, cores)
    near = swap(to_near, "sx", 0)
    far = swap(to_far, "sx", 1)
    weight, edge, offsets = ((9, 256, 256), BF), ((3, 256, 256), BF), ((16, 128, 128), BF)
    w1, w1_edge, dwr = call(
        prepare_first_kernel, [weight, edge, offsets], [((2048, 128), F32)], 2, False, 1 << 27, 8
    )(w_first, down_weight)
    skip, cells = ((384, 256), BF), ((4, 8, 512), BF)
    groups = jnp.asarray(regroup(), BF)
    skip_near, skip_own, to_far, coarse_own = call(
        near_kernel,
        [skip, skip, cells, ((2, 8, 512), BF)],
        [((2, 3, 416, 256), BF), ((2, 416, 256), BF), ((512, 512), BF)],
        6,
        True,
        2 << 30,
        10,
    )(bounds, own, near, groups, w1, w1_edge, dwr)
    far_cells = swap(to_far, "sx", 1)
    skip_far, to_near = call(
        far_kernel,
        [skip, cells],
        [((1, 3, 416, 256), BF), ((1, 416, 256), BF), ((512, 256), BF)],
        7,
        True,
        1 << 30,
        10,
    )(bounds, own, far, groups, w1, w1_edge, dwr, coarse_own)
    near_cells = swap(to_near, "sx", 0)
    skip_weight, skip_edge, up_weight, up_edge, wupr = call(
        prepare_last_kernel, [weight, edge, weight, edge, offsets], [((2048, 128), F32)], 2, False, 1 << 28, 10
    )(closing_weight, w_up)
    taps = w_coarse.shape[0] * w_coarse.shape[1]
    (w_in_out,) = call(transpose_kernel, [((taps, 128, 128), BF)], [], 1, False, 1 << 28, 8)(
        w_coarse.reshape(taps, 128, 128)
    )
    shifts = [((3, 288, 512), BF), ((2, 288, 256), BF)]
    (part,) = call(skip_kernel, [((2, 256, 256), F32)], shifts, 5, True, 2 << 30, 8)(
        bounds, skip_near, skip_own, skip_far, skip_weight, skip_edge
    )
    odd_order = jnp.concatenate([near_cells, to_far[:2], to_near, far_cells], axis=0)
    even_order = jnp.concatenate([far_cells, to_near, to_far[2:], near_cells], axis=0)
    coarse = jnp.where(odd, odd_order, even_order)
    chips, cores = y_swaps(coarse[:, 2:6], coarse[:, 0:4], odd_y)
    before, after = jnp.where(odd_y, cores, chips), jnp.where(odd_y, chips, cores)
    coarse = jnp.concatenate([before, coarse[:, 0:6], after, jnp.zeros((14, 2, 512), BF)], axis=1)
    (up,) = call(
        coarse_kernel, [((288, 768), BF)], [((3, 224, 512), BF), ((512, 768), F32)], 4, True, 3 << 30, 12
    )(bounds, coarse, w_in_out, wupr, jnp.asarray(regroup().T[48:336], BF))
    (result,) = call(last_kernel, [((32, 16, 256), BF)], shifts, 4, False, 2 << 30, 12)(up, up_weight, up_edge, part)
    return result


def solution(mesh):
    return jax.shard_map(
        local,
        mesh=mesh,
        in_specs=(P(None, "sx", "sy"), P(), P(), P(), P(), P()),
        out_specs=P(None, "sx", "sy"),
        check_vma=False,
    )
```

```python
import jax
import jax.numpy as jnp
import numpy as np
from jax import lax
from jax.experimental import pallas as pl
from jax.experimental.pallas import tpu as pltpu
from jax.sharding import PartitionSpec as P

NZ = 16
BF = jnp.bfloat16
F32 = jnp.float32
NT = (((1,), (1,)), ((), ()))
NN = (((1,), (0,)), ((), ()))
TN = (((0,), (0,)), ((), ()))


def iota(shape, dim):
    return lax.broadcasted_iota(jnp.int32, shape, dim)


def dot(a, b, dims):
    return lax.dot_general(a, b, dims, preferred_element_type=F32)


def z_shifts(value, rows):
    z = iota(value.shape, 0) & (NZ - 1)
    before = jnp.where(z == 0, 0.0, pltpu.roll(value, 1, 0))
    after = jnp.where(z == NZ - 1, 0.0, pltpu.roll(value, rows - 1, 0))
    return before, value, after


def regroup():
    coarse, fine = np.arange(512)[:, None], np.arange(384)[None]
    y = 4 * (coarse & 7) + (coarse >> 7)
    z = 4 * (coarse >> 3 & 3) + (coarse >> 5 & 3)
    return fine == y * NZ + z


def moved(value, start, target):
    lane = iota(value.shape, 1)
    return jnp.where(lane >> 5 == target // 32, pltpu.roll(value, (target - start) % 128, 1), 0.0)


def packed(joined, tile, fifth_tile, start):
    fifth = joined[:, 128 * fifth_tile : 128 * fifth_tile + 128]
    blocks = [moved(fifth[104 * k : 104 * k + 104], start, 32 * k) for k in range(4)]
    return jnp.concatenate(
        [joined[:, 128 * tile : 128 * tile + 128], (blocks[0] + blocks[1]) + (blocks[2] + blocks[3])], axis=0
    )


def pack_kernel(bounds, own, chips, cores, joined_ref, to_near, to_far):
    odd, odd_y = bounds[8] == 1, bounds[9] == 1
    chip, core = chips[...].astype(F32), cores[...].astype(F32)
    joined = jnp.concatenate(
        [jnp.where(odd_y, core, chip), own[...].astype(F32), jnp.where(odd_y, chip, core)], axis=0
    )
    joined_ref[...] = joined.astype(BF)
    left, right = packed(joined, 0, 1, 0), packed(joined, 3, 2, 96)
    to_far[...] = jnp.where(odd, right, left).astype(BF)
    to_near[...] = jnp.where(odd, left, right).astype(BF)


def own_window(own):
    return [own[:, 128 * tile : 128 * tile + 128].astype(F32) for tile in range(4)]


def side_window(own, halo, halo_at_left):
    tiles = own_window(own)
    fifth = halo[416:520].astype(F32)
    at_end, at_start = (
        jnp.concatenate([moved(fifth, 32 * k, lane) for k in range(4)], axis=0)
        for lane in (96, 0)
    )
    close = halo[0:416].astype(F32)
    left, right = (at_end, close, tiles[0], tiles[1]), (tiles[2], tiles[3], close, at_start)
    return [jnp.where(halo_at_left, one, other) for one, other in zip(left, right)]


def fill_edges(before, after, rows, target):
    lane = iota((rows, 128), 1)
    both = jnp.where(lane >= 96, before, jnp.where(lane < 32, after, 0.0))
    low, middle, high = z_shifts(both, rows)
    target[:, 0:128] = (pltpu.roll(low, 32, 1) + pltpu.roll(middle, 96, 1)).astype(BF)
    target[:, 128:256] = pltpu.roll(high, 32, 1).astype(BF)


def fine_groups(windows, bounds, to_groups, w1, w1_edge, dwr, skip_refs, coarse_refs, vz, edges, grouped):
    parts = 2 // len(windows)
    rows = 384 // parts
    chains = [(k, rows * part) for k in range(len(windows)) for part in range(parts)]
    for k, (tiles, _) in enumerate(windows):
        for half in range(2):
            for oz, shifted in enumerate(z_shifts(tiles[1 + half], 416)):
                vz[k, oz, :, 128 * half : 128 * half + 128] = shifted.astype(BF)
        fill_edges(tiles[0], tiles[3], 416, edges.at[k])
    summed = [jnp.zeros((rows, 256), F32) for _ in chains]
    for oy in range(3):
        for oz in range(4):
            for c, (k, start) in enumerate(chains):
                here = slice(start + 16 * oy, start + 16 * oy + rows)
                if oz < 3:
                    summed[c] += dot(vz[k, oz, here], w1[3 * oy + oz], NT)
                else:
                    summed[c] += dot(edges[k, here], w1_edge[oy], NT)
    for c, (k, start) in enumerate(chains):
        y = ((iota((rows, 256), 0) + start) >> 4) - 4
        x = (iota((rows, 256), 1) >> 5) + windows[k][1]
        inside = (y >= bounds[2]) & (y <= bounds[3]) & (x >= bounds[0]) & (x <= bounds[1])
        skip_refs[k][start : start + rows] = jnp.where(inside, jnp.maximum(summed[c], 0.0), 0.0).astype(BF)
    for k in range(len(windows)):
        grouped[:, 256 * k : 256 * k + 256] = dot(to_groups[...], skip_refs[k][...], NN).astype(BF)
    count = 2 * len(windows)
    coarse = jnp.zeros((32 * count, 128), F32)
    for i in range(0, 16, 2):
        pieces = []
        for a in range(count):
            lanes = slice(128 * a, 128 * a + 128)
            pieces.append(
                jnp.concatenate([grouped[32 * i : 32 * i + 32, lanes], grouped[32 * i + 32 : 32 * i + 64, lanes]], axis=1)
            )
        coarse += dot(
            jnp.concatenate(pieces, axis=0), jnp.concatenate([dwr[i], dwr[i + 1]], axis=0), NN
        )
    for a in range(count):
        for target, first_a in coarse_refs[a // 2]:
            for z in range(4):
                cell = coarse[32 * a + 8 * z : 32 * a + 8 * z + 8].astype(BF)
                target[first_a + a % 2, :, 128 * z : 128 * z + 128] = cell


def near_kernel(bounds, own, near, groups, w1, w1_edge, dwr, skip_near, skip_own, to_far, coarse_own, vz, edges, grouped):
    odd = bounds[8] == 1
    first_near, first_own = 2 - 2 * bounds[8], 2 * bounds[8]
    windows = ((side_window(own, near, odd), jnp.where(odd, -4, 12)), (own_window(own), 4))
    coarse = ([(to_far, first_near)], [(to_far, first_own), (coarse_own, 0)])
    fine_groups(windows, bounds, groups, w1, w1_edge, dwr, (skip_near, skip_own), coarse, vz, edges, grouped)


def far_kernel(bounds, own, far, groups, w1, w1_edge, dwr, coarse_own, skip_far, to_near, vz, edges, grouped):
    to_near[pl.ds(2 - 2 * bounds[8], 2)] = coarse_own[...]
    even = bounds[8] == 0
    windows = ((side_window(own, far, even), jnp.where(even, -4, 12)),)
    coarse = ([(to_near, 2 * bounds[8])],)
    fine_groups(windows, bounds, groups, w1, w1_edge, dwr, (skip_far,), coarse, vz, edges, grouped)


def fill_shifts(tile_of, middle, edges):
    for tile in range(1, 5):
        for oz, shifted in enumerate(z_shifts(tile_of(tile), 288)):
            middle[oz, :, 128 * tile - 128 : 128 * tile] = shifted.astype(BF)
    for g in range(2):
        fill_edges(tile_of(2 * g), tile_of(2 * g + 3), 288, edges.at[g])


def closing_sums(weight, weight_edge, middle, edges):
    summed = [jnp.zeros((256, 256), F32) for _ in range(2)]
    for oy in range(3):
        rows = slice(16 * oy, 16 * oy + 256)
        for oz in range(4):
            for g in range(2):
                if oz < 3:
                    summed[g] += dot(middle[oz, rows, 256 * g : 256 * g + 256], weight[3 * oy + oz], NT)
                else:
                    summed[g] += dot(edges[g, rows], weight_edge[oy], NT)
    return summed


def skip_kernel(bounds, near, own, far, weight, weight_edge, out_ref, middle, edges):
    odd = bounds[8] == 1

    def tile_of(tile):
        group, half = divmod(tile, 2)
        here = slice(128 * half, 128 * half + 128)
        if group == 1:
            return own[48:336, here].astype(F32)
        first, second = near[48:336, here].astype(F32), far[48:336, here].astype(F32)
        return jnp.where(odd, first, second) if group == 0 else jnp.where(odd, second, first)

    fill_shifts(tile_of, middle, edges)
    for g, summed in enumerate(closing_sums(weight, weight_edge, middle, edges)):
        out_ref[g] = summed


def transpose_kernel(source, target):
    identity = jnp.where(iota((128, 128), 0) == iota((128, 128), 1), 1.0, 0.0).astype(BF)
    for t in range(0, source.shape[0], 4):
        pair = dot(identity, jnp.concatenate([source[t], source[t + 1]], axis=0), NT).astype(BF)
        target[t], target[t + 1] = pair[:, :128], pair[:, 128:]
        target[t + 2], target[t + 3] = source[t + 2].T, source[t + 3].T


def coarse_kernel(bounds, coarse_ref, w_coarse, wupr, from_groups, up, state, raw):
    value = coarse_ref[...].reshape(224, 512).astype(F32)
    for layer in range(4):
        rows_in = (14 - 2 * layer) * 16
        rows = rows_in - 32
        state[0, :rows_in] = value.astype(BF)
        state[1, :rows_in] = pltpu.roll(value, rows_in - 1, 0).astype(BF)
        state[2, :rows_in] = pltpu.roll(value, rows_in - 2, 0).astype(BF)
        low = jnp.zeros((rows, 256), F32)
        high = jnp.zeros((rows, 256), F32)
        zero = jnp.zeros((128, 128), BF)
        for oa in range(3):
            for ob in range(3):
                w = [w_coarse[27 * layer + 9 * oa + 3 * ob + oz] for oz in range(3)]
                one, two = jnp.concatenate([w[1], w[0]], axis=1), jnp.concatenate([w[2], w[1]], axis=1)
                w_low = jnp.concatenate([one, two, jnp.concatenate([zero, w[2]], axis=1)], axis=0)
                w_high = jnp.concatenate([jnp.concatenate([w[0], zero], axis=1), one, two], axis=0)
                low += dot(state[ob, 16 * oa : 16 * oa + rows, 0:384], w_low, NN)
                high += dot(state[ob, 16 * oa : 16 * oa + rows, 128:512], w_high, NN)
        index = iota((rows, 128), 0)
        a = (index >> 4) - 4 + layer
        b = (index & 15) - 4 + layer
        kept = (a >= bounds[4]) & (a <= bounds[5]) & (b < 8 - layer) & (b >= bounds[6]) & (b <= bounds[7])
        value = jnp.concatenate(
            [
                jnp.where(kept, jnp.maximum(half[:, side : side + 128], 0.0), 0.0)
                for half in (low, high)
                for side in (0, 128)
            ],
            axis=1,
        )
        value = value.astype(BF).astype(F32)
    cells = jnp.concatenate(
        [value[16 * a : 16 * a + 8, 128 * z : 128 * z + 128] for z in range(4) for a in range(6)], axis=0
    ).astype(BF)
    for i in range(0, 16, 2):
        pair = dot(cells, jnp.concatenate([wupr[i], wupr[i + 1]], axis=0), NT)
        for half in range(2):
            for z in range(4):
                for a in range(6):
                    raw[32 * (i + half) + 8 * z : 32 * (i + half) + 8 * z + 8, 128 * a : 128 * a + 128] = pair[
                        48 * z + 8 * a : 48 * z + 8 * a + 8, 128 * half : 128 * half + 128
                    ]
    for g in range(3):
        lanes = slice(256 * g, 256 * g + 256)
        up[:, lanes] = dot(from_groups[...], raw[:, lanes].astype(BF), NN).astype(BF)


def last_kernel(up, weight, weight_edge, part_ref, out_ref, middle, edges):
    fill_shifts(lambda tile: up[:, 128 * tile : 128 * tile + 128].astype(F32), middle, edges)
    row, column = iota((256, 256), 0), iota((256, 256), 1)
    to_channels = jnp.where(column == ((row & 7) << 5) + (row >> 3), 1.0, 0.0).astype(BF)
    for g, summed in enumerate(closing_sums(weight, weight_edge, middle, edges)):
        total = (summed + part_ref[g]).astype(BF)
        out_ref[:, 8 * g : 8 * g + 8, :] = dot(to_channels, total, NT).reshape(32, 8, 256).astype(BF)


def banded(source, target, edge_target, channels):
    inputs = source.shape[2]
    repeat = iota((inputs, 256), 0) - channels == iota((inputs, 256), 1) & 31
    repeat = jnp.where(repeat, 1.0, 0.0).astype(BF)
    plane = iota((32, 256), 1) >> 5
    for oy in range(3):
        before = after = jnp.zeros((32, 256), F32)
        for oz in range(3):
            t = 3 * oy + oz
            tiled = dot(jnp.concatenate([source[t], source[t + 9], source[t + 18]], axis=0), repeat, NN)
            for x in range(8):
                rows = jnp.where(plane == x + 1, tiled[64:], 0.0)
                rows = jnp.where(plane == x, tiled[32:64], rows)
                rows = jnp.where(plane == x - 1, tiled[:32], rows)
                target[t, 32 * x : 32 * x + 32] = rows.astype(BF)
            before = jnp.where(plane == 2 * oz, tiled[:32], before)
            after = jnp.where(plane == 2 * oz + 1, tiled[64:], after)
        edge_target[oy, 0:32] = before.astype(BF)
        edge_target[oy, 32:224] = jnp.zeros((192, 256), BF)
        edge_target[oy, 224:256] = after.astype(BF)


def by_offset(tall, target):
    for i in range(16):
        for x in range(4):
            target[i, 32 * x : 32 * x + 32] = tall[pl.ds(16 * x + i, 32, stride=64), :].astype(BF)


def prepare_first_kernel(first, w1, w1_edge):
    banded(first, w1, w1_edge, 0)


def prepare_down_kernel(down, dwr, tall):
    tall[...] = down[...].astype(F32)
    by_offset(tall, dwr)


def prepare_last_kernel(closing, up, skip_weight, skip_edge, up_weight, up_edge, wupr, tall):
    banded(closing, skip_weight, skip_edge, 0)
    banded(closing, up_weight, up_edge, 32)
    for k in range(16):
        tall[128 * k : 128 * k + 128] = up[:, 128 * k : 128 * k + 128].astype(F32).T
    by_offset(tall, wupr)


VMEM = pl.BlockSpec(memory_space=pltpu.VMEM)
SMEM = pl.BlockSpec(memory_space=pltpu.SMEM)


def call(body, shapes, scratch, n_in, scalars, flops, limit):
    return pl.pallas_call(
        body,
        out_shape=[jax.ShapeDtypeStruct(s, t) for s, t in shapes],
        in_specs=([SMEM] if scalars else []) + [VMEM] * n_in,
        out_specs=[VMEM] * len(shapes),
        scratch_shapes=[pltpu.VMEM(s, t) for s, t in scratch],
        compiler_params=pltpu.CompilerParams(vmem_limit_bytes=limit << 20),
        cost_estimate=pl.CostEstimate(flops=flops, bytes_accessed=4 << 20, transcendentals=0),
    )


def ones_where(condition):
    return jnp.where(condition, 1.0, 0.0).astype(BF)


def place_own():
    r, lane = iota((512, 512), 0), iota((512, 512), 1)
    return ones_where((lane & 31 == r >> 4) & (lane >> 5 == r & 15))


def swap(array, axis, start):
    pairs = [(i, i + 1) for i in range(start, lax.axis_size(axis) - 1, 2)]
    return lax.ppermute(array, axis, pairs + [(j, i) for i, j in pairs])


def y_swaps(bottom, top, odd_y):
    chips = swap(jnp.where(odd_y, top, bottom), "sy", 1)
    cores = swap(jnp.where(odd_y, bottom, top), "sy", 0)
    return chips, cores


def local(volume, w_first, down_weight, w_coarse, w_up, closing_weight):
    ix, iy = lax.axis_index("sx"), lax.axis_index("sy")
    first_x, last_x = ix == 0, ix == lax.axis_size("sx") - 1
    first_y, last_y = iy == 0, iy == lax.axis_size("sy") - 1
    bounds = jnp.stack(
        [
            jnp.where(first_x, 0, -99),
            jnp.where(last_x, 15, 99),
            jnp.where(first_y, 0, -99),
            jnp.where(last_y, 15, 99),
            jnp.where(first_x, 0, -99),
            jnp.where(last_x, 3, 99),
            jnp.where(first_y, 0, -99),
            jnp.where(last_y, 3, 99),
            ix & 1,
            iy & 1,
        ]
    ).astype(jnp.int32)
    odd = (ix & 1) == 1
    own = dot(volume.reshape(512, 256), place_own(), TN).astype(BF)
    odd_y = (iy & 1) == 1
    chips, cores = y_swaps(own[0:80], own[176:256], odd_y)
    own, to_near, to_far = call(
        pack_kernel, [((416, 512), BF), ((520, 128), BF), ((520, 128), BF)], [], 3, True, 1 << 20, 8
    )(bounds, own, chips, cores)
    near = swap(to_near, "sx", 0)
    far = swap(to_far, "sx", 1)
    weight, edge, offsets = ((9, 256, 256), BF), ((3, 256, 256), BF), ((16, 128, 128), BF)
    (dwr,) = call(prepare_down_kernel, [offsets], [((2048, 128), F32)], 1, False, 1 << 26, 8)(down_weight)
    w1, w1_edge = call(prepare_first_kernel, [weight, edge], [], 1, False, 1 << 27, 8)(w_first)
    skip, cells = ((384, 256), BF), ((4, 8, 512), BF)
    groups = jnp.asarray(regroup(), BF)
    skip_near, skip_own, to_far, coarse_own = call(
        near_kernel,
        [skip, skip, cells, ((2, 8, 512), BF)],
        [((2, 3, 416, 256), BF), ((2, 416, 256), BF), ((512, 512), BF)],
        6,
        True,
        2 << 30,
        10,
    )(bounds, own, near, groups, w1, w1_edge, dwr)
    far_cells = swap(to_far, "sx", 1)
    skip_far, to_near = call(
        far_kernel,
        [skip, cells],
        [((1, 3, 416, 256), BF), ((1, 416, 256), BF), ((512, 256), BF)],
        7,
        True,
        1 << 30,
        10,
    )(bounds, own, far, groups, w1, w1_edge, dwr, coarse_own)
    near_cells = swap(to_near, "sx", 0)
    skip_weight, skip_edge, up_weight, up_edge, wupr = call(
        prepare_last_kernel, [weight, edge, weight, edge, offsets], [((2048, 128), F32)], 2, False, 1 << 28, 10
    )(closing_weight, w_up)
    taps = w_coarse.shape[0] * w_coarse.shape[1]
    (w_in_out,) = call(transpose_kernel, [((taps, 128, 128), BF)], [], 1, False, 1 << 28, 8)(
        w_coarse.reshape(taps, 128, 128)
    )
    shifts = [((3, 288, 512), BF), ((2, 288, 256), BF)]
    (part,) = call(skip_kernel, [((2, 256, 256), F32)], shifts, 5, True, 2 << 30, 8)(
        bounds, skip_near, skip_own, skip_far, skip_weight, skip_edge
    )
    odd_order = jnp.concatenate([near_cells, to_far[:2], to_near, far_cells], axis=0)
    even_order = jnp.concatenate([far_cells, to_near, to_far[2:], near_cells], axis=0)
    coarse = jnp.where(odd, odd_order, even_order)
    chips, cores = y_swaps(coarse[:, 2:6], coarse[:, 0:4], odd_y)
    before, after = jnp.where(odd_y, cores, chips), jnp.where(odd_y, chips, cores)
    coarse = jnp.concatenate([before, coarse[:, 0:6], after, jnp.zeros((14, 2, 512), BF)], axis=1)
    (up,) = call(
        coarse_kernel, [((288, 768), BF)], [((3, 224, 512), BF), ((512, 768), F32)], 4, True, 3 << 30, 12
    )(bounds, coarse, w_in_out, wupr, jnp.asarray(regroup().T[48:336], BF))
    (result,) = call(last_kernel, [((32, 16, 256), BF)], shifts, 4, False, 2 << 30, 12)(up, up_weight, up_edge, part)
    return result


def solution(mesh):
    return jax.shard_map(
        local,
        mesh=mesh,
        in_specs=(P(None, "sx", "sy"), P(), P(), P(), P(), P()),
        out_specs=P(None, "sx", "sy"),
        check_vma=False,
    )
```
